32 devices in a mesh: groups: 2 (over y), blk: 4 (over z), head: 4 (over x, core).
Axes of the slice: x: 2, y: 2, z: 4, core: 2. Of those that a mesh axis runs over, the one named last changes fastest.
Arguments:
- ctx_query: bfloat16 [4096, 8192], P(('groups', 'blk'), 'head'), parts along dimension 0, may hold values from -5 to 5
- ctx_key: bfloat16 [4096, 1024], P(('groups', 'blk'), 'head'), parts along dimension 0, may hold values from -5 to 5
- ctx_value: bfloat16 [4096, 1024], P(('groups', 'blk'), 'head'), parts along dimension 0, may hold values from -4.5 to 4.5
- opt_query: bfloat16 [128, 8192], P(('groups', 'blk'), 'head'), parts along dimension 0, may hold values from -5 to 5
- opt_owner: int32 [128], P('groups'), parts along dimension 0, may hold values from 0 to 3, as said below
- opt_slot: int32 [128], P('groups'), parts along dimension 0, may hold values from 0 to 31, as said below
- opt_length: int32 [128], P('groups'), parts along dimension 0, may hold values from 512 to 2048
Outputs:
- ctx_out: bfloat16 [4096, 8192], P(('groups', 'blk'), 'head'), parts along dimension 0
- opt_out: bfloat16 [256, 8192], P(('groups', 'blk'), 'head'), parts along dimension 0
The draws below stay inside these ranges and needn't reach their ends.
There are 2 independent parts, one for each index of `groups`. The reference program is written for one: setup_inputs(seed, part) draws one part's arguments, and reference() takes and returns one part's arrays. A program takes and returns all parts, laid end to end along the dimension named above; each array names one. Nothing has to cross between parts.
Inputs may be any that keep to these rules, and one draw needn't show every extreme that they name: `opt_owner`: each option token has its own pair of owner block and slot; no block owns more than 32 option tokens, and one block owns exactly 32. `opt_slot`: slots of one owner are distinct.
All inputs are finite; a program needn't handle non-finite values.
Results may differ from the reference program's by a relative error of at most 0.017.
Values may be sent and summed in bfloat16 or wider, within the bound.
A program may use at most 64 MiB of HBM per device.

```python
import jax
import jax.numpy as jnp
from jax import lax

HD = 128
HQ = 64
KVH = 8
BLK = 512
CAP = 32
CTX = 2048
OPTS = 64
N_BLK = 4


def base_values(key, rows, cols):
    return jnp.clip(jax.random.normal(key, (rows, cols), jnp.float32), -4.5, 4.5)


def draw_ctx_key(key, part):
    values = base_values(jax.random.fold_in(key, 11), CTX, KVH * HD)
    return values.astype(jnp.bfloat16)


def draw_ctx_query(key, part):
    values = base_values(jax.random.fold_in(key, 12), CTX, HQ * HD)
    return values.astype(jnp.bfloat16)


def draw_opt_query(key, part):
    values = jax.random.uniform(jax.random.fold_in(key, 13), (OPTS, HQ * HD), jnp.float32, -5.0, 5.0)
    return values.astype(jnp.bfloat16)


def option_places(key):
    base = jax.random.fold_in(key, 21)
    slot_count = N_BLK * CAP
    full_owner = jax.random.randint(jax.random.fold_in(base, 1), (), 0, N_BLK)
    owner_bias = jax.random.randint(jax.random.fold_in(base, 2), (N_BLK,), 0, 3)
    noise = jax.random.randint(jax.random.fold_in(base, 3), (slot_count,), 0, 65536)
    slot_ids = jnp.arange(slot_count, dtype=jnp.int32)
    owners = slot_ids // CAP
    score = noise + owner_bias[owners] * 32768 + (owners == full_owner).astype(jnp.int32) * 262144
    ranked = jnp.argsort(-(score * slot_count + slot_ids))
    chosen = ranked[:OPTS].astype(jnp.int32)
    shuffle = jax.random.permutation(jax.random.fold_in(base, 4), OPTS)
    chosen = chosen[shuffle]
    return ((chosen // CAP).astype(jnp.int32), (chosen % CAP).astype(jnp.int32))


def draw_opt_owner(key, part):
    return option_places(key)[0]


def draw_opt_slot(key, part):
    return option_places(key)[1]


def place_ends(drawn, own_key, low, high):
    place = [jax.random.randint(jax.random.fold_in(own_key, axis), (), 0, length) for axis, length in enumerate(drawn.shape)]
    main_axis = drawn.shape.index(max(drawn.shape))
    beside = place[:main_axis] + [(place[main_axis] + 1) % drawn.shape[main_axis]] + place[main_axis + 1:]
    return drawn.at[tuple(place)].set(low).at[tuple(beside)].set(high)


def levels(stream_key, shape, pieces, low, high):
    level, own = 1.0, jax.random.fold_in(stream_key, 6)
    for axis_at, blocks in pieces:
        draws = jnp.exp(jax.random.uniform(jax.random.fold_in(own, axis_at), (blocks,), jnp.float32, low / len(pieces), high / len(pieces)))
        level = level * jnp.repeat(draws, shape[axis_at] // blocks).reshape([-1 if axis == axis_at else 1 for axis in range(len(shape))])
    return level


def normal_values(rng, extent, deviation, limit, split=(), held_as=jnp.bfloat16):
    values = deviation * jax.random.normal(rng, extent, jnp.float32)
    if split:
        values = values * levels(rng, extent, split, -0.22, 0.18)
    return jnp.clip(values, -limit, limit).astype(held_as)


def setup_inputs(seed: int = 0, part: int = 0) -> dict:
    key_list = jax.random.split(jax.random.key(seed), 8)
    own_keys = jax.random.split(jax.random.fold_in(key_list[7], part), 8)
    return {
        "ctx_query": draw_ctx_query(jax.random.fold_in(jax.random.fold_in(key_list[7], part), 71), part),
        "ctx_key": draw_ctx_key(jax.random.fold_in(jax.random.fold_in(key_list[7], part), 71), part),
        "ctx_value": normal_values(own_keys[2], (CTX, KVH * HD), 1.0, 4.5, ((0, 4), (1, 4))),
        "opt_query": draw_opt_query(jax.random.fold_in(jax.random.fold_in(key_list[7], part), 71), part),
        "opt_owner": draw_opt_owner(jax.random.fold_in(jax.random.fold_in(key_list[7], part), 71), part),
        "opt_slot": draw_opt_slot(jax.random.fold_in(jax.random.fold_in(key_list[7], part), 71), part),
        "opt_length": place_ends(jax.random.randint(own_keys[6], (OPTS,), BLK, CTX + 1), jax.random.fold_in(own_keys[6], 1), BLK, CTX).astype(jnp.int32),
    }


def reference(ctx_query, ctx_key, ctx_value, opt_query, opt_owner, opt_slot, opt_length):
    group_size = HQ // KVH
    scale = HD ** -0.5
    high = lax.Precision.HIGHEST
    query_all = ctx_query.reshape(N_BLK, BLK, HQ, HD)
    key_all = ctx_key.reshape(N_BLK, BLK, KVH, HD)
    value_all = ctx_value.reshape(N_BLK, BLK, KVH, HD)
    anchor_key = jnp.repeat(key_all[0], group_size, axis=1).astype(jnp.float32)
    anchor_value = jnp.repeat(value_all[0], group_size, axis=1).astype(jnp.float32)
    spots = jnp.arange(BLK, dtype=jnp.int32)
    causal = spots[:, None] >= spots[None, :]

    def first_phase(index):
        query_blk = query_all[index].astype(jnp.float32)
        key_blk = jnp.repeat(key_all[index], group_size, axis=1).astype(jnp.float32)
        value_blk = jnp.repeat(value_all[index], group_size, axis=1).astype(jnp.float32)
        local = jnp.einsum('thd,shd->hts', query_blk, key_blk, precision=high) * scale
        local = jnp.where(causal[None], local, -1e30)
        remote = jnp.einsum('thd,shd->hts', query_blk, anchor_key, precision=high) * scale
        remote = jnp.where(index > 0, remote, -1e30)
        top = jnp.maximum(jnp.max(local, axis=2), jnp.max(remote, axis=2))
        e_local = jnp.exp(local - top[..., None])
        e_remote = jnp.exp(remote - top[..., None])
        total = jnp.sum(e_local, axis=2) + jnp.sum(e_remote, axis=2)
        acc = jnp.einsum('hts,shd->thd', e_local.astype(jnp.bfloat16).astype(jnp.float32), value_blk, precision=high)
        acc = acc + jnp.einsum('hts,shd->thd', e_remote.astype(jnp.bfloat16).astype(jnp.float32), anchor_value, precision=high)
        return (acc / total.T[:, :, None]).astype(jnp.bfloat16)

    ctx_out = lax.map(first_phase, jnp.arange(N_BLK, dtype=jnp.int32)).reshape(CTX, HQ * HD)

    option_q = opt_query.reshape(OPTS, HQ, HD).astype(jnp.float32)

    def second_phase(index):
        key_blk = jnp.repeat(key_all[index], group_size, axis=1).astype(jnp.float32)
        value_blk = jnp.repeat(value_all[index], group_size, axis=1).astype(jnp.float32)
        scores = jnp.einsum('ihd,shd->his', option_q, key_blk, precision=high) * scale
        count = jnp.clip(opt_length - index * BLK, 0, BLK)
        visible = spots[None, :] < count[:, None]
        scores = jnp.where(visible[None], scores, -1e30)
        top = jnp.max(scores, axis=2)
        expo = jnp.exp(scores - top[..., None])
        total = jnp.sum(expo, axis=2)
        acc = jnp.einsum('his,shd->ihd', expo.astype(jnp.bfloat16).astype(jnp.float32), value_blk, precision=high)
        live = count > 0
        part = jnp.where(live[:, None, None], acc / total.T[:, :, None], 0.0).astype(jnp.bfloat16)
        stat = jnp.where(live[:, None], (top + jnp.log(total)).T, -1e30)
        return part, stat

    parts, stats = lax.map(second_phase, jnp.arange(N_BLK, dtype=jnp.int32))
    top_all = jnp.max(stats, axis=0)
    weight = jnp.exp(stats - top_all[None])
    merged = jnp.sum(weight[..., None] * parts.astype(jnp.float32), axis=0) / jnp.sum(weight, axis=0)[..., None]
    where_to = (opt_owner * CAP + opt_slot).astype(jnp.int32)
    opt_out = jnp.zeros((CAP * N_BLK, HQ * HD), jnp.bfloat16).at[where_to].set(merged.reshape(OPTS, HQ * HD).astype(jnp.bfloat16))
    return ctx_out, opt_out
```

```python
import functools
import math

import jax
import jax.numpy as jnp
from jax import lax
from jax.experimental import pallas as pl
from jax.experimental.pallas import tpu as pltpu
from jax.sharding import PartitionSpec as P

HD = 128
HQ = 64
KVH = 8
CAP = 32
GROUP = HQ // KVH
MESH = pl.DeviceIdType.MESH
NEG = -1e30
LN2 = math.log(2.0)
COEF = HD**-0.5 / LN2
PAIR = 2
QUAD = 4
HALVES = 2
PIECES = 4
VR = HD + 16


def dot_nt(a, b):
    return lax.dot_general(a, b, (((1,), (1,)), ((), ())), preferred_element_type=jnp.float32)


def dot_nn(a, b, precision=None):
    return lax.dot_general(
        a, b, (((1,), (0,)), ((), ())), preferred_element_type=jnp.float32, precision=precision
    )


def staged(count, scores, soften, gather):
    for k in range(count + 2):
        if k < count:
            scores(k)
        if 0 <= k - 1 < count:
            soften(k - 1)
        if 0 <= k - 2 < count:
            gather(k - 2)


def attend(
    n,
    q_hbm, k_hbm, v_hbm, oq_hbm, len_hbm, owner_hbm, slot_hbm,
    ctx_ref, rx_p, rx_s, mine_ref,
    q_ref, k_ref, v_ref, vt_ref, ak_ref, av_ref, avt_ref, oq_ref, acc_ref, m_ref,
    part_ref, stat_ref, pbuf, sbuf, place_ref,
    place_sem, q_sem, k_sem, v_sem, o_sem,
    oq_send, oq_recv, ou_send, ou_recv, ak_send, ak_recv, av_send, av_recv,
    p_send, p_recv, s_send, s_recv,
):
    me = lax.axis_index("blk")
    rows = q_ref.shape[0]
    heads = q_ref.shape[1] // HD
    kvs = k_ref.shape[1] // HD
    entry = oq_hbm.shape[0]
    opts = oq_ref.shape[0]
    pairs = heads // PAIR
    tile = rows // 2
    span_rows = rows // HALVES
    chunk = span_rows // PIECES
    chunks = kvs * HALVES * PIECES

    def q_copy(i):
        cols = pl.ds(pl.multiple_of(i * PAIR * HD, PAIR * HD), PAIR * HD)
        return pltpu.make_async_copy(q_hbm.at[:, cols], q_ref.at[:, cols], q_sem.at[i])

    k_copy = pltpu.make_async_copy(k_hbm, k_ref, k_sem)
    v_copy = pltpu.make_async_copy(v_hbm, v_ref, v_sem)
    own = pl.ds(pl.multiple_of(me * entry, entry), entry)
    o_copy = pltpu.make_async_copy(oq_hbm, oq_ref.at[own], o_sem)

    place_copies = [
        pltpu.make_async_copy(src, place_ref.at[pl.ds(8 * i, 1)], place_sem.at[i])
        for i, src in enumerate((len_hbm, owner_hbm, slot_hbm))
    ]
    barrier = pltpu.get_barrier_semaphore()
    for step in range(1, n):
        pl.semaphore_signal(
            barrier, inc=1, device_id={"blk": lax.rem(me + step, n)}, device_id_type=MESH
        )
    k_copy.start()
    q_copy(0).start()
    v_copy.start()
    for i in range(1, pairs):
        q_copy(i).start()
    o_copy.start()
    for copy in place_copies:
        copy.start()
    pl.semaphore_wait(barrier, n - 1)

    def oq_down(step):
        return pltpu.make_async_remote_copy(
            src_ref=oq_hbm,
            dst_ref=oq_ref.at[own],
            send_sem=oq_send.at[step - 1],
            recv_sem=oq_recv.at[step - 1],
            device_id={"blk": lax.rem(me - step + n, n)},
            device_id_type=MESH,
        )

    def oq_up(step):
        at = lax.rem(me - step + 1 + n, n)
        span = pl.ds(pl.multiple_of(at * entry, entry), entry)
        return pltpu.make_async_remote_copy(
            src_ref=oq_hbm if step == 1 else oq_ref.at[span],
            dst_ref=oq_ref.at[span],
            send_sem=ou_send.at[step - 1],
            recv_sem=ou_recv.at[step - 1],
            device_id={"blk": lax.rem(me + 1, n)},
            device_id_type=MESH,
        )

    def oq_up_arrived(step):
        @pl.when(me >= step)
        def _():
            oq_up(step).wait_recv()

    def oq_up_start(step):
        @pl.when((me >= step - 1) & (me < n - 1))
        def _():
            oq_up(step).start()

    up = lax.rem(me + 1, n)

    def anchor_copies(c, first):
        g = c // (HALVES * PIECES)
        r = lax.rem(c, HALVES * PIECES)
        span = pl.ds(pl.multiple_of(r * chunk, chunk), chunk)
        cols = pl.ds(pl.multiple_of(g * HD, HD), HD)
        key_from = k_hbm if first else ak_ref
        value_from = v_hbm if first else av_ref
        return (
            pltpu.make_async_remote_copy(
                src_ref=key_from.at[span, cols],
                dst_ref=ak_ref.at[span, cols],
                send_sem=ak_send.at[c],
                recv_sem=ak_recv.at[c],
                device_id={"blk": up},
                device_id_type=MESH,
            ),
            pltpu.make_async_remote_copy(
                src_ref=value_from.at[span, cols],
                dst_ref=av_ref.at[span, cols],
                send_sem=av_send.at[c],
                recv_sem=av_recv.at[c],
                device_id={"blk": up},
                device_id_type=MESH,
            ),
        )

    oq_up_start(1)

    @pl.when(me == 0)
    def _():
        def send(c, carry):
            for copy in anchor_copies(c, True):
                copy.start()
            return carry

        lax.fori_loop(0, chunks, send, 0)

    for step in range(1, n):
        @pl.when(me >= step)
        def _():
            oq_down(step).start()

    def forward(c):
        for copy in anchor_copies(c, False):
            copy.wait_recv()

        @pl.when(me < n - 1)
        def _():
            for copy in anchor_copies(c, False):
                copy.start()

    def head_cols(h):
        return pl.ds(pl.multiple_of(h * HD, HD), HD)

    ones = jnp.ones((VR - HD, rows), jnp.bfloat16)
    k_copy.wait()
    v_copy.wait()
    for g in range(kvs):
        vt_ref[g, :HD, :] = v_ref[:, g * HD : (g + 1) * HD].T
        vt_ref[g, HD:, :] = ones
        avt_ref[g, HD:, :] = ones

    causal = lax.broadcasted_iota(jnp.int32, (tile, tile), 0) <= lax.broadcasted_iota(
        jnp.int32, (tile, tile), 1
    )

    def local_heads(hs):
        units = [(h, t) for h in hs for t in range(2)]
        raw, tops, probs = {}, {}, {}

        def scores(u):
            h, t = units[u]
            query = q_ref[pl.ds(t * tile, tile), head_cols(h)]
            score = dot_nt(k_ref[pl.ds(0, (t + 1) * tile), head_cols(h // GROUP)], query)
            parts = [score[j * tile : (j + 1) * tile] for j in range(t + 1)]
            parts[t] = jnp.where(causal, parts[t], NEG)
            top = functools.reduce(jnp.maximum, [jnp.max(x, axis=0, keepdims=True) for x in parts])
            tops[u] = top * COEF
            raw[u] = parts

        def soften(u):
            probs[u] = [jnp.exp2(x * COEF - tops[u]).astype(jnp.bfloat16) for x in raw.pop(u)]

        def gather(u):
            h, t = units[u]
            span = pl.ds(t * tile, tile)
            prob = jnp.concatenate(probs.pop(u), axis=0)
            acc_ref[h, :, span] = dot_nn(vt_ref[h // GROUP, :, pl.ds(0, (t + 1) * tile)], prob)
            m_ref[h, :, span] = jnp.broadcast_to(tops[u], (8, tile))

        staged(len(units), scores, soften, gather)

    def finish(h, span, acc):
        ctx_ref[span, head_cols(h)] = (acc[:HD] * (1.0 / acc[HD : HD + 1])).T.astype(jnp.bfloat16)

    def anchor_heads(hs, half, last):
        units = [(h, t) for h in hs for t in range(2)]
        keys = pl.ds(half * span_rows, span_rows)
        raw, tops, probs = {}, {}, {}

        def scores(u):
            h, t = units[u]
            span = pl.ds(t * tile, tile)
            raw[u] = dot_nt(ak_ref[keys, head_cols(h // GROUP)], q_ref[span, head_cols(h)])
            top = jnp.max(raw[u], axis=0, keepdims=True) * COEF
            tops[u] = jnp.maximum(top, m_ref[h, pl.ds(0, 1), span])

        def soften(u):
            probs[u] = jnp.exp2(raw.pop(u) * COEF - tops[u]).astype(jnp.bfloat16)

        def gather(u):
            h, t = units[u]
            span = pl.ds(t * tile, tile)
            alpha = jnp.exp2(m_ref[h, pl.ds(0, 1), span] - tops[u])
            acc = dot_nn(avt_ref[h // GROUP, :, keys], probs.pop(u)) + alpha * acc_ref[h, :, span]
            if last:
                finish(h, span, acc)
            else:
                acc_ref[h, :, span] = acc
                m_ref[h, :, span] = jnp.broadcast_to(tops[u], (8, tile))

        staged(len(units), scores, soften, gather)

    for copy in place_copies:
        copy.wait()
    length = place_ref[pl.ds(0, 1), :].astype(jnp.float32)
    dest = place_ref[pl.ds(8, 1), :] * CAP + place_ref[pl.ds(16, 1), :]

    def opt_attend(queries, counts, key, value_t):
        size = queries.shape[0]
        stacked = jnp.concatenate([queries[:, j * HD : (j + 1) * HD] for j in range(GROUP)], axis=0)
        score = dot_nt(key, stacked)
        if counts is not None:
            spot = lax.broadcasted_iota(jnp.int32, score.shape, 0).astype(jnp.float32)
            score = jnp.where(spot < counts, score, NEG)
        top = jnp.max(score, axis=0, keepdims=True) * COEF
        acc = dot_nn(value_t, jnp.exp2(score * COEF - top).astype(jnp.bfloat16))
        total = acc[HD : HD + 1]
        part = acc[:HD] * (1.0 / total)
        stat = top * LN2 + jnp.log(total)
        if counts is not None:
            live = counts > 0.0
            part = jnp.where(live, part, 0.0)
            stat = jnp.where(live, stat, NEG)
        part = part.T.astype(jnp.bfloat16)
        stat = jnp.broadcast_to(stat, (HD, stat.shape[1])).T
        return (
            [part[j * size : (j + 1) * size] for j in range(GROUP)],
            [stat[j * size : (j + 1) * size] for j in range(GROUP)],
        )

    step_rows = min(opts, 64)
    lane_opts = GROUP * step_rows

    def options_group(g):
        lanes = lax.broadcasted_iota(jnp.int32, (step_rows, HD), 1)
        for base in range(0, opts, step_rows):
            span = pl.ds(base, step_rows)
            pick = lax.broadcasted_iota(jnp.int32, (opts, lane_opts), 0) - base
            pick = pick == lax.rem(lax.broadcasted_iota(jnp.int32, (opts, lane_opts), 1), step_rows)
            spread = dot_nn(
                jnp.broadcast_to(length, (8, opts)), pick.astype(jnp.float32), lax.Precision.HIGHEST
            )
            counts = jnp.clip(spread[:1] - (me * rows).astype(jnp.float32), 0.0, float(rows))
            queries = oq_ref[span, pl.ds(g * GROUP * HD, GROUP * HD)]
            parts, tops = opt_attend(queries, counts, k_ref[:, pl.ds(g * HD, HD)], vt_ref[g])
            stats = jnp.zeros((step_rows, HD), jnp.float32) if g == 0 else stat_ref[span, :]
            for j in range(GROUP):
                h = g * GROUP + j
                part_ref[span, pl.ds(h * HD, HD)] = parts[j]
                stats = jnp.where(lanes == h, tops[j], stats)
            stat_ref[span, :] = stats

    slots = lax.broadcasted_iota(jnp.int32, (CAP, opts), 0)
    mine = (slots + me * CAP == dest).astype(jnp.float32)
    mine_ref[...] = jnp.broadcast_to(jnp.sum(mine, axis=1, keepdims=True), (CAP, HD))

    def options_scatter():
        for d in range(n):
            hot = (slots + d * CAP == dest).astype(jnp.float32)
            span = pl.ds(d * CAP, CAP)
            pbuf[span, :] = dot_nn(hot.astype(jnp.bfloat16), part_ref[...]).astype(jnp.bfloat16)
            sbuf[span, :] = dot_nn(hot, stat_ref[...], lax.Precision.HIGHEST)

    def part_copies(step):
        to = lax.rem(me + step, n)
        span = pl.ds(pl.multiple_of(to * CAP, CAP), CAP)
        return (
            pltpu.make_async_remote_copy(
                src_ref=pbuf.at[span],
                dst_ref=rx_p.at[me],
                send_sem=p_send.at[step - 1],
                recv_sem=p_recv.at[step - 1],
                device_id={"blk": to},
                device_id_type=MESH,
            ),
            pltpu.make_async_remote_copy(
                src_ref=sbuf.at[span],
                dst_ref=rx_s.at[me],
                send_sem=s_send.at[step - 1],
                recv_sem=s_recv.at[step - 1],
                device_id={"blk": to},
                device_id_type=MESH,
            ),
        )

    def options_anchor(g, key_of, value_of):
        hot = mine.astype(jnp.bfloat16)
        lanes = lax.broadcasted_iota(jnp.int32, (CAP, HD), 1)
        queries = dot_nn(hot, oq_ref[:, pl.ds(g * GROUP * HD, GROUP * HD)]).astype(jnp.bfloat16)
        parts, tops = opt_attend(queries, None, key_of[:, pl.ds(g * HD, HD)], value_of[g])
        stats = jnp.zeros((CAP, HD), jnp.float32) if g == 0 else rx_s[0]
        for j in range(GROUP):
            h = g * GROUP + j
            rx_p[0, :, pl.ds(h * HD, HD)] = parts[j]
            stats = jnp.where(lanes == h, tops[j], stats)
        rx_s[0] = stats

    def local_pair(i, carry):
        q_copy(i).wait()
        local_heads([i * PAIR + j for j in range(PAIR)])

        @pl.when((i == max(pairs - 3, 0)) & (me > 1))
        def _():
            oq_up_arrived(1)
            oq_up_start(2)

        return carry

    lax.fori_loop(0, pairs, local_pair, 0)

    def send_parts(upward):
        for step in range(1, n):
            @pl.when((me + step < n) if upward else (me + step >= n))
            def _():
                for copy in part_copies(step):
                    copy.start()

    def oq_rest():
        @pl.when(me == 1)
        def _():
            oq_up_arrived(1)
            oq_up_start(2)

        for step in range(2, n):
            oq_up_arrived(step)
            if step < n - 1:
                oq_up_start(step + 1)
        o_copy.wait()
        for step in range(1, n):
            @pl.when(me + step < n)
            def _():
                oq_down(step).wait_recv()

    oq_rest()

    @pl.when(me == 0)
    def _():
        def whole(h, carry):
            for t in range(2):
                span = pl.ds(t * tile, tile)
                finish(h, span, acc_ref[h, :, span])
            return carry

        lax.fori_loop(0, heads, whole, 0)
        for g in range(kvs):
            options_anchor(g, k_ref, vt_ref)

    @pl.when(me > 0)
    def _():
        done = 0
        for g in range(kvs):
            options_group(g)
            for c in range(done, min(done + 1, PIECES)):
                forward(c)
            done = min(done + 1, PIECES)
        options_scatter()
        send_parts(False)
        for c in range(done, PIECES):
            forward(c)
        own_slots = pl.ds(pl.multiple_of(me * CAP, CAP), CAP)
        rx_p[me] = pbuf[own_slots, :]
        rx_s[me] = sbuf[own_slots, :]

        per = GROUP // QUAD
        ahead = PIECES // per

        def group(g, carry):
            for half in range(HALVES):
                keys = pl.ds(half * span_rows, span_rows)
                avt_ref[g, :HD, keys] = av_ref[keys, head_cols(g)].T

                def quad(i, carry):
                    anchor_heads(
                        [g * GROUP + i * QUAD + j for j in range(QUAD)], half, half == HALVES - 1
                    )
                    base = (g * HALVES + half + 1) * PIECES + i * ahead

                    @pl.when(base < chunks)
                    def _():
                        for j in range(ahead):
                            forward(base + j)

                    return carry

                lax.fori_loop(0, per, quad, 0)

                if half == HALVES - 2:
                    @pl.when(g == kvs - 1)
                    def _():
                        send_parts(True)

            return carry

        lax.fori_loop(0, kvs, group, 0)
        for g in range(kvs):
            options_anchor(g, ak_ref, avt_ref)

    for step in range(1, n):
        @pl.when(lax.rem(me - step + n, n) > 0)
        def _():
            for copy in part_copies(step):
                copy.wait_recv()

    for step in range(1, n):
        @pl.when(me >= step)
        def _():
            oq_down(step).wait_send()

        @pl.when((me >= step - 1) & (me < n - 1))
        def _():
            oq_up(step).wait_send()

    @pl.when(me == 0)
    def _():
        def drain(c, carry):
            for copy in anchor_copies(c, True):
                copy.wait_send()
            return carry

        lax.fori_loop(0, chunks, drain, 0)

    @pl.when((me > 0) & (me < n - 1))
    def _():
        def drain(c, carry):
            for copy in anchor_copies(c, False):
                copy.wait_send()
            return carry

        lax.fori_loop(0, chunks, drain, 0)

    @pl.when(me > 0)
    def _():
        for step in range(1, n):
            for copy in part_copies(step):
                copy.wait_send()


def merge(n, ctx_ref, rx_p, rx_s, mine_ref, ctx_hbm, opt_ref, sem):
    copy = pltpu.make_async_copy(ctx_ref, ctx_hbm, sem)
    copy.start()
    heads = opt_ref.shape[1] // HD
    top = rx_s[0]
    for b in range(1, n):
        top = jnp.maximum(top, rx_s[b])
    total = jnp.zeros_like(top)
    for b in range(n):
        total = total + jnp.exp(rx_s[b] - top)
    occupied = mine_ref[...] > 0.0
    for h in range(heads):
        cols = pl.ds(h * HD, HD)
        merged = jnp.zeros((CAP, HD), jnp.float32)
        for b in range(n):
            weight = jnp.exp(rx_s[b, :, pl.ds(h, 1)] - top[:, h : h + 1])
            merged = merged + weight * rx_p[b, :, cols].astype(jnp.float32)
        merged = merged / total[:, h : h + 1]
        opt_ref[:, cols] = jnp.where(occupied, merged, 0.0).astype(jnp.bfloat16)
    copy.wait()


def body(ctx_query, ctx_key, ctx_value, opt_query, opt_owner, opt_slot, opt_length):
    n = lax.axis_size("blk")
    rows, width = ctx_query.shape
    heads = width // HD
    kvs = ctx_key.shape[1] // HD
    opts = opt_length.shape[0]
    chunks = HALVES * PIECES * kvs
    bf16, f32 = jnp.bfloat16, jnp.float32
    dma = pltpu.SemaphoreType.DMA
    hbm = pl.BlockSpec(memory_space=pltpu.HBM)
    vmem = pl.BlockSpec(memory_space=pltpu.VMEM)
    length, owner, slot = (x.reshape(1, opts) for x in (opt_length, opt_owner, opt_slot))
    kept = 2 * width * (rows + n * CAP) + 4 * HD * CAP * (n + 1)
    ctx, parts, stats, mine = pl.pallas_call(
        functools.partial(attend, n),
        out_shape=(
            pltpu.VMEM((rows, width), bf16),
            pltpu.VMEM((n, CAP, width), bf16),
            pltpu.VMEM((n, CAP, HD), f32),
            pltpu.VMEM((CAP, HD), f32),
        ),
        in_specs=[hbm] * 7,
        out_specs=(vmem, vmem, vmem, vmem),
        scratch_shapes=[
            pltpu.VMEM((rows, width), bf16),
            pltpu.VMEM((rows, kvs * HD), bf16),
            pltpu.VMEM((rows, kvs * HD), bf16),
            pltpu.VMEM((kvs, VR, rows), bf16),
            pltpu.VMEM((rows, kvs * HD), bf16),
            pltpu.VMEM((rows, kvs * HD), bf16),
            pltpu.VMEM((kvs, VR, rows), bf16),
            pltpu.VMEM((opts, width), bf16),
            pltpu.VMEM((heads, VR, rows), f32),
            pltpu.VMEM((heads, 8, rows), f32),
            pltpu.VMEM((opts, width), bf16),
            pltpu.VMEM((opts, HD), f32),
            pltpu.VMEM((n * CAP, width), bf16),
            pltpu.VMEM((n * CAP, HD), f32),
            pltpu.VMEM((24, opts), jnp.int32),
            dma((3,)), dma((heads // PAIR,)), dma(()), dma(()), dma(()),
            dma((n - 1,)), dma((n - 1,)), dma((n - 1,)), dma((n - 1,)),
            dma((chunks,)), dma((chunks,)), dma((chunks,)), dma((chunks,)),
            dma((n - 1,)), dma((n - 1,)), dma((n - 1,)), dma((n - 1,)),
        ],
        compiler_params=pltpu.CompilerParams(
            collective_id=0, has_side_effects=True, vmem_limit_bytes=65100 * 1024 - kept
        ),
        name="star",
    )(ctx_query, ctx_key, ctx_value, opt_query, length, owner, slot)
    return pl.pallas_call(
        functools.partial(merge, n),
        out_shape=(
            jax.ShapeDtypeStruct((rows, width), bf16),
            jax.ShapeDtypeStruct((CAP, width), bf16),
        ),
        in_specs=[vmem] * 4,
        out_specs=(hbm, vmem),
        scratch_shapes=[dma(())],
        compiler_params=pltpu.CompilerParams(vmem_limit_bytes=16 * 1024 * 1024),
        name="merge",
    )(ctx, parts, stats, mine)


def solution(mesh):
    return jax.shard_map(
        body,
        mesh=mesh,
        in_specs=(
            P(("groups", "blk"), "head"),
            P(("groups", "blk"), "head"),
            P(("groups", "blk"), "head"),
            P(("groups", "blk"), "head"),
            P("groups"),
            P("groups"),
            P("groups"),
        ),
        out_specs=(P(("groups", "blk"), "head"), P(("groups", "blk"), "head")),
        check_vma=False,
    )
```

```python
import functools
import math

import jax
import jax.numpy as jnp
from jax import lax
from jax.experimental import pallas as pl
from jax.experimental.pallas import tpu as pltpu
from jax.sharding import PartitionSpec as P

HD = 128
HQ = 64
KVH = 8
CAP = 32
GROUP = HQ // KVH
MESH = pl.DeviceIdType.MESH
NEG = -1e30
LN2 = math.log(2.0)
COEF = HD**-0.5 / LN2
PAIR = 2
HALVES = 2
PIECES = 4
VR = HD + 16
WRITES = 8
LEAD = 2


def dot_nt(a, b):
    return lax.dot_general(a, b, (((1,), (1,)), ((), ())), preferred_element_type=jnp.float32)


def dot_nn(a, b, precision=None):
    return lax.dot_general(
        a, b, (((1,), (0,)), ((), ())), preferred_element_type=jnp.float32, precision=precision
    )


def staged(count, scores, soften, gather):
    for k in range(count + 2):
        if k < count:
            scores(k)
        if 0 <= k - 1 < count:
            soften(k - 1)
        if 0 <= k - 2 < count:
            gather(k - 2)


def attend(
    n,
    q_hbm, k_hbm, v_hbm, oq_hbm, len_hbm, owner_hbm, slot_hbm,
    ctx_ref, rx_p, rx_s, mine_ref,
    q_ref, k_ref, v_ref, vt_ref, ak_ref, av_ref, avt_ref, oq_ref, acc_ref, m_ref,
    raw_a, raw_b, prob_a, prob_b, top_a, top_b, part_ref, stat_ref, pbuf, sbuf, up_p, up_s, place_ref,
    place_sem, q_sem, k_sem, v_sem, o_sem,
    oq_send, oq_recv, oz_send, oz_recv, ak_send, ak_recv, av_send, av_recv,
    p_send, p_recv, s_send, s_recv, pu_send, pu_recv, su_send, su_recv, low_sem, high_sem,
):
    me = lax.axis_index("blk")
    rows = q_ref.shape[0]
    heads = q_ref.shape[1] // HD
    kvs = k_ref.shape[1] // HD
    entry = oq_hbm.shape[0]
    opts = oq_ref.shape[0]
    pairs = heads // PAIR
    tile = rows // 2
    span_rows = rows // HALVES
    chunk = span_rows // PIECES
    chunks = kvs * HALVES * PIECES

    def q_copy(i):
        cols = pl.ds(pl.multiple_of(i * PAIR * HD, PAIR * HD), PAIR * HD)
        return pltpu.make_async_copy(q_hbm.at[:, cols], q_ref.at[:, cols], q_sem.at[i])

    k_copy = pltpu.make_async_copy(k_hbm, k_ref, k_sem)
    v_copy = pltpu.make_async_copy(v_hbm, v_ref, v_sem)
    own = pl.ds(pl.multiple_of(me * entry, entry), entry)
    o_copy = pltpu.make_async_copy(oq_hbm, oq_ref.at[own], o_sem)

    place_copies = [
        pltpu.make_async_copy(src, place_ref.at[pl.ds(8 * i, 1)], place_sem.at[i])
        for i, src in enumerate((len_hbm, owner_hbm, slot_hbm))
    ]
    barrier = pltpu.get_barrier_semaphore()
    up = lax.rem(me + 1, n)
    below = lax.rem(me - 1 + n, n)

    @pl.when(me < n - 1)
    def _():
        pl.semaphore_signal(barrier, inc=1, device_id={"blk": up}, device_id_type=MESH)

    @pl.when(me > 0)
    def _():
        pl.semaphore_signal(barrier, inc=1, device_id={"blk": below}, device_id_type=MESH)

    k_copy.start()
    q_copy(0).start()
    v_copy.start()
    for i in range(1, pairs):
        q_copy(i).start()
    o_copy.start()
    for copy in place_copies:
        copy.start()

    @pl.when((me > 0) & (me < n - 1))
    def _():
        pl.semaphore_wait(barrier, 2)

    @pl.when((me == 0) | (me == n - 1))
    def _():
        pl.semaphore_wait(barrier, 1)

    def oq_copy(step):
        return pltpu.make_async_remote_copy(
            src_ref=oq_hbm,
            dst_ref=oq_ref.at[own],
            send_sem=oq_send.at[step - 1],
            recv_sem=oq_recv.at[step - 1],
            device_id={"blk": lax.rem(me - step + n, n)},
            device_id_type=MESH,
        )

    first_rows = pl.ds(0, entry)

    def oq_first(index, to, relay):
        return pltpu.make_async_remote_copy(
            src_ref=oq_ref.at[first_rows] if relay else oq_hbm,
            dst_ref=oq_ref.at[first_rows],
            send_sem=oz_send.at[index],
            recv_sem=oz_recv,
            device_id={"blk": to},
            device_id_type=MESH,
        )

    def anchor_copies(c, first):
        g = c // (HALVES * PIECES)
        r = lax.rem(c, HALVES * PIECES)
        span = pl.ds(pl.multiple_of(r * chunk, chunk), chunk)
        cols = pl.ds(pl.multiple_of(g * HD, HD), HD)
        key_from = k_hbm if first else ak_ref
        value_from = v_hbm if first else av_ref
        return (
            pltpu.make_async_remote_copy(
                src_ref=key_from.at[span, cols],
                dst_ref=ak_ref.at[span, cols],
                send_sem=ak_send.at[c],
                recv_sem=ak_recv.at[c],
                device_id={"blk": up},
                device_id_type=MESH,
            ),
            pltpu.make_async_remote_copy(
                src_ref=value_from.at[span, cols],
                dst_ref=av_ref.at[span, cols],
                send_sem=av_send.at[c],
                recv_sem=av_recv.at[c],
                device_id={"blk": up},
                device_id_type=MESH,
            ),
        )

    def send_anchor(low, high):
        def send(c, carry):
            for copy in anchor_copies(c, True):
                copy.start()
            return carry

        lax.fori_loop(low, high, send, 0)

    @pl.when(me == 0)
    def _():
        oq_first(0, up, False).start()
        send_anchor(0, LEAD)

    @pl.when(me > 1)
    def _():
        pl.semaphore_wait(low_sem, 1)

    @pl.when((me > 0) & (me < n - 1))
    def _():
        pl.semaphore_signal(low_sem, inc=1, device_id={"blk": up}, device_id_type=MESH)

    @pl.when(me < n - 2)
    def _():
        pl.semaphore_wait(high_sem, 1)

    @pl.when((me > 0) & (me < n - 1))
    def _():
        pl.semaphore_signal(high_sem, inc=1, device_id={"blk": below}, device_id_type=MESH)

    @pl.when(me == 0)
    def _():
        if n > 2:
            oq_first(1, n - 1, False).start()
        send_anchor(LEAD, chunks)

    @pl.when(me > 0)
    def _():
        for step in range(n - 1, 0, -1):
            oq_copy(step).start()

    def forward(c):
        for copy in anchor_copies(c, False):
            copy.wait_recv()

        @pl.when(me < n - 1)
        def _():
            for copy in anchor_copies(c, False):
                copy.start()

    def head_cols(h):
        return pl.ds(pl.multiple_of(h * HD, HD), HD)

    ones = jnp.ones((VR - HD, rows), jnp.bfloat16)
    k_copy.wait()
    v_copy.wait()
    for g in range(kvs):
        vt_ref[g, :HD, :] = v_ref[:, g * HD : (g + 1) * HD].T
        vt_ref[g, HD:, :] = ones
        avt_ref[g, HD:, :] = ones

    causal = lax.broadcasted_iota(jnp.int32, (tile, tile), 0) <= lax.broadcasted_iota(
        jnp.int32, (tile, tile), 1
    )

    def local_heads(hs):
        units = [(h, t) for h in hs for t in range(2)]
        raw, tops, probs = {}, {}, {}

        def scores(u):
            h, t = units[u]
            query = q_ref[pl.ds(t * tile, tile), head_cols(h)]
            score = dot_nt(k_ref[pl.ds(0, (t + 1) * tile), head_cols(h // GROUP)], query)
            parts = [score[j * tile : (j + 1) * tile] for j in range(t + 1)]
            parts[t] = jnp.where(causal, parts[t], NEG)
            top = functools.reduce(jnp.maximum, [jnp.max(x, axis=0, keepdims=True) for x in parts])
            tops[u] = top * COEF
            raw[u] = parts

        def soften(u):
            probs[u] = [jnp.exp2(x * COEF - tops[u]).astype(jnp.bfloat16) for x in raw.pop(u)]

        def gather(u):
            h, t = units[u]
            span = pl.ds(t * tile, tile)
            prob = jnp.concatenate(probs.pop(u), axis=0)
            acc_ref[h, :, span] = dot_nn(vt_ref[h // GROUP, :, pl.ds(0, (t + 1) * tile)], prob)
            m_ref[h, :, span] = jnp.broadcast_to(tops[u], (8, tile))

        staged(len(units), scores, soften, gather)

    def finish(h, span, acc):
        ctx_ref[span, head_cols(h)] = (acc[:HD] * (1.0 / acc[HD : HD + 1])).T.astype(jnp.bfloat16)

    units = heads * HALVES
    per = GROUP // 2

    def unit_place(u):
        block = u // GROUP
        g = block // HALVES
        half = lax.rem(block, HALVES)
        keys = pl.ds(pl.multiple_of(half * span_rows, span_rows), span_rows)
        return g, g * GROUP + lax.rem(u, GROUP), keys

    def unit_scores(u, raw, top):
        g, h, keys = unit_place(jnp.minimum(u, units - 1))
        for t in range(2):
            span = pl.ds(t * tile, tile)
            score = dot_nt(ak_ref[keys, head_cols(g)], q_ref[span, head_cols(h)])
            raw[:, span] = score
            high = jnp.max(score, axis=0, keepdims=True) * COEF
            high = jnp.maximum(high, m_ref[h, pl.ds(0, 1), span])
            top[pl.ds(0, 8), span] = jnp.broadcast_to(high, (8, tile))

    def unit_soften(raw, top, prob):
        for t in range(2):
            span = pl.ds(t * tile, tile)
            high = top[pl.ds(0, 1), span]
            prob[:, span] = jnp.exp2(raw[:, span] * COEF - high).astype(jnp.bfloat16)
        top[pl.ds(8, 8), :] = top[pl.ds(0, 8), :]

    def unit_gather(u, prob, top, last):
        g, h, keys = unit_place(jnp.maximum(u, 0))
        slot = jnp.where(u < 0, heads, h)
        for t in range(2):
            span = pl.ds(t * tile, tile)
            high = top[pl.ds(8, 1), span]
            alpha = jnp.exp2(m_ref[slot, pl.ds(0, 1), span] - high)
            acc = dot_nn(avt_ref[g, :, keys], prob[:, span]) + alpha * acc_ref[slot, :, span]
            if last:
                finish(h, span, acc)
            else:
                acc_ref[slot, :, span] = acc
                m_ref[slot, :, span] = jnp.broadcast_to(high, (8, tile))

    def trip(i, last):
        unit_gather(2 * i - 2, prob_a, top_a, last)
        unit_soften(raw_b, top_b, prob_b)
        unit_scores(2 * i, raw_a, top_a)
        unit_gather(2 * i - 1, prob_b, top_b, last)
        unit_soften(raw_a, top_a, prob_a)
        unit_scores(2 * i + 1, raw_b, top_b)

    for copy in place_copies:
        copy.wait()
    length = place_ref[pl.ds(0, 1), :].astype(jnp.float32)
    dest = place_ref[pl.ds(8, 1), :] * CAP + place_ref[pl.ds(16, 1), :]

    def opt_attend(queries, counts, key, value_t):
        size = queries.shape[0]
        stacked = jnp.concatenate([queries[:, j * HD : (j + 1) * HD] for j in range(GROUP)], axis=0)
        score = dot_nt(key, stacked)
        if counts is not None:
            spot = lax.broadcasted_iota(jnp.int32, score.shape, 0).astype(jnp.float32)
            score = jnp.where(spot < counts, score, NEG)
        top = jnp.max(score, axis=0, keepdims=True) * COEF
        acc = dot_nn(value_t, jnp.exp2(score * COEF - top).astype(jnp.bfloat16))
        total = acc[HD : HD + 1]
        part = acc[:HD] * (1.0 / total)
        stat = top * LN2 + jnp.log(total)
        if counts is not None:
            live = counts > 0.0
            part = jnp.where(live, part, 0.0)
            stat = jnp.where(live, stat, NEG)
        part = part.T.astype(jnp.bfloat16)
        stat = jnp.broadcast_to(stat, (HD, stat.shape[1])).T
        return (
            [part[j * size : (j + 1) * size] for j in range(GROUP)],
            [stat[j * size : (j + 1) * size] for j in range(GROUP)],
        )

    step_rows = min(opts, 64)
    lane_opts = GROUP * step_rows

    def options_group(g):
        lanes = lax.broadcasted_iota(jnp.int32, (step_rows, HD), 1)
        for base in range(0, opts, step_rows):
            span = pl.ds(base, step_rows)
            pick = lax.broadcasted_iota(jnp.int32, (opts, lane_opts), 0) - base
            pick = pick == lax.rem(lax.broadcasted_iota(jnp.int32, (opts, lane_opts), 1), step_rows)
            spread = dot_nn(
                jnp.broadcast_to(length, (8, opts)), pick.astype(jnp.float32), lax.Precision.HIGHEST
            )
            counts = jnp.clip(spread[:1] - (me * rows).astype(jnp.float32), 0.0, float(rows))
            queries = oq_ref[span, pl.ds(g * GROUP * HD, GROUP * HD)]
            parts, tops = opt_attend(queries, counts, k_ref[:, pl.ds(g * HD, HD)], vt_ref[g])
            stats = jnp.zeros((step_rows, HD), jnp.float32) if g == 0 else stat_ref[span, :]
            for j in range(GROUP):
                h = g * GROUP + j
                part_ref[span, pl.ds(h * HD, HD)] = parts[j]
                stats = jnp.where(lanes == h, tops[j], stats)
            stat_ref[span, :] = stats

    slots = lax.broadcasted_iota(jnp.int32, (CAP, opts), 0)
    mine = (slots + me * CAP == dest).astype(jnp.float32)
    mine_ref[...] = jnp.broadcast_to(jnp.sum(mine, axis=1, keepdims=True), (CAP, HD))

    def options_scatter():
        for d in range(n):
            hot = (slots + d * CAP == dest).astype(jnp.float32)
            span = pl.ds(d * CAP, CAP)
            pbuf[span, :] = dot_nn(hot.astype(jnp.bfloat16), part_ref[...]).astype(jnp.bfloat16)
            sbuf[span, :] = dot_nn(hot, stat_ref[...], lax.Precision.HIGHEST)

    def down_copies(step):
        to = lax.rem(me - step + n, n)
        span = pl.ds(pl.multiple_of(to * CAP, CAP), CAP)
        return (
            pltpu.make_async_remote_copy(
                src_ref=pbuf.at[span],
                dst_ref=rx_p.at[me],
                send_sem=p_send.at[step - 1],
                recv_sem=p_recv.at[step - 1],
                device_id={"blk": to},
                device_id_type=MESH,
            ),
            pltpu.make_async_remote_copy(
                src_ref=sbuf.at[span],
                dst_ref=rx_s.at[me],
                send_sem=s_send.at[step - 1],
                recv_sem=s_recv.at[step - 1],
                device_id={"blk": to},
                device_id_type=MESH,
            ),
        )

    def up_copies(d, final):
        span = pl.ds(d * CAP, CAP)
        return (
            pltpu.make_async_remote_copy(
                src_ref=pbuf.at[span],
                dst_ref=rx_p.at[me] if final else up_p.at[d],
                send_sem=pu_send.at[d],
                recv_sem=pu_recv.at[d],
                device_id={"blk": up},
                device_id_type=MESH,
            ),
            pltpu.make_async_remote_copy(
                src_ref=sbuf.at[span],
                dst_ref=rx_s.at[me] if final else up_s.at[d],
                send_sem=su_send.at[d],
                recv_sem=su_recv.at[d],
                device_id={"blk": up},
                device_id_type=MESH,
            ),
        )

    def send_down():
        for step in range(n - 1, 0, -1):
            @pl.when(me >= step)
            def _():
                for copy in down_copies(step):
                    copy.start()

    def combine(d):
        span = pl.ds(d * CAP, CAP)
        low, own_stat = up_s[d], sbuf[span, :]
        top = jnp.maximum(low, own_stat)
        low, own_stat = jnp.exp(low - top), jnp.exp(own_stat - top)
        total = low + own_stat
        sbuf[span, :] = top + jnp.log(total)
        low, own_stat = low / total, own_stat / total
        for h in range(heads):
            cols = pl.ds(h * HD, HD)
            mixed = low[:, h : h + 1] * up_p[d, :, cols].astype(jnp.float32)
            mixed = mixed + own_stat[:, h : h + 1] * pbuf[span, cols].astype(jnp.float32)
            pbuf[span, cols] = mixed.astype(jnp.bfloat16)

    def send_up_first():
        for d in range(n - 1, 2, -1):
            @pl.when(me == 1)
            def _():
                for copy in up_copies(d, False):
                    copy.start()

    def send_up_rest():
        for d in range(n - 1, 1, -1):
            @pl.when((me > 1) & (me < d))
            def _():
                for copy in up_copies(d, False):
                    copy.wait_recv()
                combine(d)

            @pl.when((me > 1) & (me < d - 1))
            def _():
                for copy in up_copies(d, False):
                    copy.start()

            @pl.when((me > 1) & (me == d - 1))
            def _():
                for copy in up_copies(d, True):
                    copy.start()

    def send_up_last():
        for copy in up_copies(min(2, n - 1), True):
            copy.start()

    def options_anchor(g, key_of, value_of):
        hot = mine.astype(jnp.bfloat16)
        lanes = lax.broadcasted_iota(jnp.int32, (CAP, HD), 1)
        queries = dot_nn(hot, oq_ref[:, pl.ds(pl.multiple_of(g * GROUP * HD, GROUP * HD), GROUP * HD)]).astype(jnp.bfloat16)
        parts, tops = opt_attend(queries, None, key_of[:, head_cols(g)], value_of[g])
        stats = rx_s[0]
        for j in range(GROUP):
            h = g * GROUP + j
            rx_p[0, :, head_cols(h)] = parts[j]
            stats = jnp.where(lanes == h, tops[j], stats)
        rx_s[0] = stats

    def local_pair(i, carry):
        q_copy(i).wait()
        local_heads([i * PAIR + j for j in range(PAIR)])

        @pl.when((i >= pairs - 2) & (me == 1))
        def _():
            forward(i - (pairs - 2))

        return carry

    lax.fori_loop(0, pairs, local_pair, 0)

    def oq_rest():
        o_copy.wait()
        for step in range(1, n):
            @pl.when(lax.rem(me + step, n) > 0)
            def _():
                oq_copy(step).wait_recv()

        @pl.when((me > 1) & (me < n - 1))
        def _():
            forward(0)
            forward(1)

        @pl.when(me > 0)
        def _():
            oq_first(0, below, True).wait_recv()

        @pl.when(me > 2)
        def _():
            oq_first(0, below, True).start()

    oq_rest()

    @pl.when(me == 0)
    def _():
        def whole(h, carry):
            for t in range(2):
                span = pl.ds(t * tile, tile)
                finish(h, span, acc_ref[h, :, span])
            return carry

        lax.fori_loop(0, heads, whole, 0)
        rx_s[0] = jnp.zeros_like(rx_s[0])
        for g in range(kvs):
            options_anchor(g, k_ref, vt_ref)

    @pl.when(me > 0)
    def _():
        early = jnp.where(me < n - 1, 2, 0)
        for g in range(kvs):
            options_group(g)

            @pl.when(early + g < PIECES)
            def _():
                forward(early + g)

        options_scatter()
        send_down()

        def rest(c, carry):
            forward(c)
            return carry

        lax.fori_loop(jnp.minimum(early + kvs, PIECES), PIECES, rest, 0)
        own_slots = pl.ds(pl.multiple_of(me * CAP, CAP), CAP)
        rx_p[me] = pbuf[own_slots, :]
        rx_s[me] = sbuf[own_slots, :]
        for b in range(1, n - 2):
            @pl.when(b < me - 1)
            def _():
                rx_p[b] = jnp.zeros_like(rx_p[b])
                rx_s[b] = jnp.full_like(rx_s[b], NEG)

        rx_s[0] = jnp.zeros_like(rx_s[0])

        def anchor_step(i, carry):
            @pl.when((lax.rem(i, per) == 0) & (2 * i < units))
            def _():
                g, _, keys = unit_place(2 * i)
                avt_ref[g, :HD, keys] = av_ref[keys, head_cols(g)].T

            last = lax.rem((jnp.maximum(i, 1) - 1) // per, HALVES) == HALVES - 1

            @pl.when(last)
            def _():
                trip(i, True)

            @pl.when(jnp.logical_not(last))
            def _():
                trip(i, False)

            @pl.when(i < chunks - PIECES)
            def _():
                forward(PIECES + i)

            @pl.when((me == 1) & (i == chunks - PIECES))
            def _():
                send_up_first()

            @pl.when((me == 1) & (me < n - 1) & (i == units // 2 - 2))
            def _():
                send_up_last()

            @pl.when((me > 1) & (me < n - 1) & (i == units // 2 - 1))
            def _():
                send_up_rest()

            @pl.when((lax.rem(i, per * HALVES) == 0) & (i > 0))
            def _():
                options_anchor(i // (per * HALVES) - 1, ak_ref, avt_ref)

            return carry

        lax.fori_loop(0, units // 2 + 1, anchor_step, 0)

    for step in range(1, n):
        @pl.when(me + step < n)
        def _():
            for copy in down_copies(step):
                copy.wait_recv()

    for d in range(2, n):
        @pl.when(me == d)
        def _():
            for copy in up_copies(d, True):
                copy.wait_recv()

    @pl.when(me > 0)
    def _():
        for step in range(1, n):
            oq_copy(step).wait_send()

    @pl.when((me == 0) | (me > 2))
    def _():
        oq_first(0, below, True).wait_send()

    if n > 2:
        @pl.when(me == 0)
        def _():
            oq_first(1, n - 1, False).wait_send()

    @pl.when(me == 0)
    def _():
        def drain(c, carry):
            for copy in anchor_copies(c, True):
                copy.wait_send()
            return carry

        lax.fori_loop(0, chunks, drain, 0)

    @pl.when((me > 0) & (me < n - 1))
    def _():
        def drain(c, carry):
            for copy in anchor_copies(c, False):
                copy.wait_send()
            return carry

        lax.fori_loop(0, chunks, drain, 0)

    for step in range(1, n):
        @pl.when(me >= step)
        def _():
            for copy in down_copies(step):
                copy.wait_send()

    for d in range(2, n):
        @pl.when((me > 0) & (me < d))
        def _():
            for copy in up_copies(d, False):
                copy.wait_send()


def merge(n, ctx_ref, rx_p, rx_s, mine_ref, ctx_hbm, opt_ref, sem):
    part = ctx_ref.shape[0] // WRITES
    copies = [
        pltpu.make_async_copy(
            ctx_ref.at[pl.ds(i * part, part)], ctx_hbm.at[pl.ds(i * part, part)], sem.at[i]
        )
        for i in range(WRITES)
    ]
    for copy in copies:
        copy.start()
    heads = opt_ref.shape[1] // HD
    top = rx_s[0]
    for b in range(1, n):
        top = jnp.maximum(top, rx_s[b])
    total = jnp.zeros_like(top)
    for b in range(n):
        total = total + jnp.exp(rx_s[b] - top)
    occupied = mine_ref[...] > 0.0
    for h in range(heads):
        cols = pl.ds(h * HD, HD)
        merged = jnp.zeros((CAP, HD), jnp.float32)
        for b in range(n):
            weight = jnp.exp(rx_s[b, :, pl.ds(h, 1)] - top[:, h : h + 1])
            merged = merged + weight * rx_p[b, :, cols].astype(jnp.float32)
        merged = merged / total[:, h : h + 1]
        opt_ref[:, cols] = jnp.where(occupied, merged, 0.0).astype(jnp.bfloat16)
    for copy in copies:
        copy.wait()


def body(ctx_query, ctx_key, ctx_value, opt_query, opt_owner, opt_slot, opt_length):
    n = lax.axis_size("blk")
    rows, width = ctx_query.shape
    heads = width // HD
    kvs = ctx_key.shape[1] // HD
    opts = opt_length.shape[0]
    chunks = HALVES * PIECES * kvs
    bf16, f32 = jnp.bfloat16, jnp.float32
    dma = pltpu.SemaphoreType.DMA
    hbm = pl.BlockSpec(memory_space=pltpu.HBM)
    vmem = pl.BlockSpec(memory_space=pltpu.VMEM)
    length, owner, slot = (x.reshape(1, opts) for x in (opt_length, opt_owner, opt_slot))
    kept = 2 * width * (rows + n * CAP) + 4 * HD * CAP * (n + 1)
    ctx, parts, stats, mine = pl.pallas_call(
        functools.partial(attend, n),
        out_shape=(
            pltpu.VMEM((rows, width), bf16),
            pltpu.VMEM((n, CAP, width), bf16),
            pltpu.VMEM((n, CAP, HD), f32),
            pltpu.VMEM((CAP, HD), f32),
        ),
        in_specs=[hbm] * 7,
        out_specs=(vmem, vmem, vmem, vmem),
        scratch_shapes=[
            pltpu.VMEM((rows, width), bf16),
            pltpu.VMEM((rows, kvs * HD), bf16),
            pltpu.VMEM((rows, kvs * HD), bf16),
            pltpu.VMEM((kvs, VR, rows), bf16),
            pltpu.VMEM((rows, kvs * HD), bf16),
            pltpu.VMEM((rows, kvs * HD), bf16),
            pltpu.VMEM((kvs, VR, rows), bf16),
            pltpu.VMEM((opts, width), bf16),
            pltpu.VMEM((heads + 1, VR, rows), f32),
            pltpu.VMEM((heads + 1, 8, rows), f32),
            pltpu.VMEM((rows // HALVES, rows), f32),
            pltpu.VMEM((rows // HALVES, rows), f32),
            pltpu.VMEM((rows // HALVES, rows), bf16),
            pltpu.VMEM((rows // HALVES, rows), bf16),
            pltpu.VMEM((16, rows), f32),
            pltpu.VMEM((16, rows), f32),
            pltpu.VMEM((opts, width), bf16),
            pltpu.VMEM((opts, HD), f32),
            pltpu.VMEM((n * CAP, width), bf16),
            pltpu.VMEM((n * CAP, HD), f32),
            pltpu.VMEM((n, CAP, width), bf16),
            pltpu.VMEM((n, CAP, HD), f32),
            pltpu.VMEM((24, opts), jnp.int32),
            dma((3,)), dma((heads // PAIR,)), dma(()), dma(()), dma(()),
            dma((n - 1,)), dma((n - 1,)), dma((2,)), dma(()),
            dma((chunks,)), dma((chunks,)), dma((chunks,)), dma((chunks,)),
            dma((n - 1,)), dma((n - 1,)), dma((n - 1,)), dma((n - 1,)),
            dma((n,)), dma((n,)), dma((n,)), dma((n,)),
            pltpu.SemaphoreType.REGULAR, pltpu.SemaphoreType.REGULAR,
        ],
        compiler_params=pltpu.CompilerParams(
            collective_id=0, has_side_effects=True, vmem_limit_bytes=65100 * 1024 - kept
        ),
        name="star",
    )(ctx_query, ctx_key, ctx_value, opt_query, length, owner, slot)
    return pl.pallas_call(
        functools.partial(merge, n),
        out_shape=(
            jax.ShapeDtypeStruct((rows, width), bf16),
            jax.ShapeDtypeStruct((CAP, width), bf16),
        ),
        in_specs=[vmem] * 4,
        out_specs=(hbm, vmem),
        scratch_shapes=[dma((WRITES,))],
        compiler_params=pltpu.CompilerParams(vmem_limit_bytes=16 * 1024 * 1024),
        name="merge",
    )(ctx, parts, stats, mine)


def solution(mesh):
    return jax.shard_map(
        body,
        mesh=mesh,
        in_specs=(
            P(("groups", "blk"), "head"),
            P(("groups", "blk"), "head"),
            P(("groups", "blk"), "head"),
            P(("groups", "blk"), "head"),
            P("groups"),
            P("groups"),
            P("groups"),
        ),
        out_specs=(P(("groups", "blk"), "head"), P(("groups", "blk"), "head")),
        check_vma=False,
    )
```

```python
import functools
import math

import jax
import jax.numpy as jnp
from jax import lax
from jax.experimental import pallas as pl
from jax.experimental.pallas import tpu as pltpu
from jax.sharding import PartitionSpec as P

HD = 128
HQ = 64
KVH = 8
CAP = 32
GROUP = HQ // KVH
MESH = pl.DeviceIdType.MESH
NEG = -1e30
LN2 = math.log(2.0)
COEF = HD**-0.5 / LN2
PAIR = 2
HALVES = 2
PIECES = 4
VR = HD + 16
PER = GROUP // 2
WRITES = 8
LEAD = 3
SPLIT = 2
LIMIT = 65100 * 1024
GREET = 0


def dot_nt(a, b):
    return lax.dot_general(a, b, (((1,), (1,)), ((), ())), preferred_element_type=jnp.float32)


def dot_nn(a, b, precision=None):
    return lax.dot_general(
        a, b, (((1,), (0,)), ((), ())), preferred_element_type=jnp.float32, precision=precision
    )


def staged(count, scores, soften, gather):
    for k in range(count + 2):
        if k < count:
            scores(k)
        if 0 <= k - 1 < count:
            soften(k - 1)
        if 0 <= k - 2 < count:
            gather(k - 2)


def attend(
    n,
    q_hbm, k_hbm, v_hbm, oq_hbm, len_hbm, owner_hbm, slot_hbm,
    ctx_ref, rx_p, rx_s, mine_ref, q_ref, ak_ref, avt_ref, acc_ref, m_ref,
    k_ref, v_ref, vt_ref, av_ref, oq_ref,
    raw_a, raw_b, prob_a, prob_b, top_a, top_b, part_ref, stat_ref, pbuf, sbuf, up_p, up_s, place_ref,
    place_sem, q_sem, k_sem, v_sem, o_sem,
    oq_send, oq_recv, ou_send, ou_recv, oz_send, oz_recv, ak_send, ak_recv, av_send, av_recv,
    p_send, p_recv, s_send, s_recv, pu_send, pu_recv, su_send, su_recv, low_sem, near_sem,
):
    me = lax.axis_index("blk")
    rows = q_ref.shape[0]
    heads = q_ref.shape[1] // HD
    kvs = k_ref.shape[1] // HD
    entry = oq_hbm.shape[0]
    opts = oq_ref.shape[0]
    pairs = heads // PAIR
    tile = rows // 2
    span_rows = rows // HALVES
    chunk = span_rows // PIECES
    chunks = kvs * HALVES * PIECES

    def q_copy(i):
        cols = pl.ds(pl.multiple_of(i * PAIR * HD, PAIR * HD), PAIR * HD)
        return pltpu.make_async_copy(q_hbm.at[:, cols], q_ref.at[:, cols], q_sem.at[i])

    k_copy = pltpu.make_async_copy(k_hbm, k_ref, k_sem)
    v_copy = pltpu.make_async_copy(v_hbm, v_ref, v_sem)
    own = pl.ds(pl.multiple_of(me * entry, entry), entry)
    o_copy = pltpu.make_async_copy(oq_hbm, oq_ref.at[own], o_sem)

    place_copies = [
        pltpu.make_async_copy(src, place_ref.at[pl.ds(8 * i, 1)], place_sem.at[i])
        for i, src in enumerate((len_hbm, owner_hbm, slot_hbm))
    ]
    barrier = pltpu.get_barrier_semaphore()
    up = lax.rem(me + 1, n)
    below = lax.rem(me - 1 + n, n)

    @pl.when(me < n - 1)
    def _():
        pl.semaphore_signal(barrier, inc=1, device_id={"blk": up}, device_id_type=MESH)

    @pl.when(me > 0)
    def _():
        pl.semaphore_signal(barrier, inc=1, device_id={"blk": below}, device_id_type=MESH)

    k_copy.start()
    q_copy(0).start()
    v_copy.start()
    for i in range(1, pairs):
        q_copy(i).start()
    o_copy.start()
    for copy in place_copies:
        copy.start()

    def oq_copy(step):
        return pltpu.make_async_remote_copy(
            src_ref=oq_hbm,
            dst_ref=oq_ref.at[own],
            send_sem=oq_send.at[step - 1],
            recv_sem=oq_recv.at[step - 1],
            device_id={"blk": lax.rem(me - step + n, n)},
            device_id_type=MESH,
        )

    def oq_up(step):
        at = lax.rem(me + 1 - step + n, n)
        span = pl.ds(pl.multiple_of(at * entry, entry), entry)
        return pltpu.make_async_remote_copy(
            src_ref=oq_hbm if step == 1 else oq_ref.at[span],
            dst_ref=oq_ref.at[span],
            send_sem=ou_send.at[step - 1],
            recv_sem=ou_recv.at[step - 1],
            device_id={"blk": up},
            device_id_type=MESH,
        )

    def oq_pass(step):
        @pl.when(me > step)
        def _():
            oq_up(step).wait_recv()

        @pl.when((me > step) & (me < n - 1))
        def _():
            oq_up(step + 1).start()

    first_rows = pl.ds(0, entry)

    hub = min(2, n - 1)

    def oq_first(index, to, relay):
        return pltpu.make_async_remote_copy(
            src_ref=oq_ref.at[first_rows] if relay else oq_hbm,
            dst_ref=oq_ref.at[first_rows],
            send_sem=oz_send.at[index],
            recv_sem=oz_recv,
            device_id={"blk": to},
            device_id_type=MESH,
        )

    def anchor_copies(c, first):
        g = c // (HALVES * PIECES)
        r = lax.rem(c, HALVES * PIECES)
        span = pl.ds(pl.multiple_of(r * chunk, chunk), chunk)
        cols = pl.ds(pl.multiple_of(g * HD, HD), HD)
        key_from = k_hbm if first else ak_ref
        value_from = v_hbm if first else av_ref
        return (
            pltpu.make_async_remote_copy(
                src_ref=key_from.at[span, cols],
                dst_ref=ak_ref.at[span, cols],
                send_sem=ak_send.at[c],
                recv_sem=ak_recv.at[c],
                device_id={"blk": up},
                device_id_type=MESH,
            ),
            pltpu.make_async_remote_copy(
                src_ref=value_from.at[span, cols],
                dst_ref=av_ref.at[span, cols],
                send_sem=av_send.at[c],
                recv_sem=av_recv.at[c],
                device_id={"blk": up},
                device_id_type=MESH,
            ),
        )

    def send_anchor(low, high):
        def send(c, carry):
            for copy in anchor_copies(c, True):
                copy.start()
            return carry

        lax.fori_loop(low, high, send, 0)

    def greet():
        @pl.when((me > 0) & (me < n - 1))
        def _():
            pl.semaphore_wait(barrier, 2)

        @pl.when((me == 0) | (me == n - 1))
        def _():
            pl.semaphore_wait(barrier, 1)

        @pl.when(me == 0)
        def _():
            send_anchor(0, LEAD)

        @pl.when(me > 1)
        def _():
            pl.semaphore_wait(low_sem, 1)

        @pl.when((me > 0) & (me < n - 1))
        def _():
            pl.semaphore_signal(low_sem, inc=1, device_id={"blk": up}, device_id_type=MESH)

        @pl.when((me == 1) & (me < n - 1))
        def _():
            pl.semaphore_signal(near_sem, inc=1, device_id={"blk": below}, device_id_type=MESH)

        if n > 2:
            @pl.when(me == 0)
            def _():
                pl.semaphore_wait(near_sem, 1)

        @pl.when(me == 0)
        def _():
            oq_first(0, hub, False).start()
            send_anchor(LEAD, chunks)

        @pl.when((me > 0) & (me < n - 1))
        def _():
            oq_up(1).start()

        for step in range(1, n):
            @pl.when(me >= step)
            def _():
                oq_copy(step).start()

    def forward(c):
        for copy in anchor_copies(c, False):
            copy.wait_recv()

        @pl.when(me < n - 1)
        def _():
            for copy in anchor_copies(c, False):
                copy.start()

    def head_cols(h):
        return pl.ds(pl.multiple_of(h * HD, HD), HD)

    ones = jnp.ones((VR - HD, rows), jnp.bfloat16)
    k_copy.wait()
    v_copy.wait()
    for g in range(kvs):
        vt_ref[g, :HD, :] = v_ref[:, g * HD : (g + 1) * HD].T
        vt_ref[g, HD:, :] = ones
        avt_ref[g, HD:, :] = ones

    causal = lax.broadcasted_iota(jnp.int32, (tile, tile), 0) <= lax.broadcasted_iota(
        jnp.int32, (tile, tile), 1
    )

    def local_heads(hs):
        units = [(h, t) for h in hs for t in range(2)]
        raw, tops, probs = {}, {}, {}

        def scores(u):
            h, t = units[u]
            query = q_ref[pl.ds(t * tile, tile), head_cols(h)]
            score = dot_nt(k_ref[pl.ds(0, (t + 1) * tile), head_cols(h // GROUP)], query)
            parts = [score[j * tile : (j + 1) * tile] for j in range(t + 1)]
            parts[t] = jnp.where(causal, parts[t], NEG)
            top = functools.reduce(jnp.maximum, [jnp.max(x, axis=0, keepdims=True) for x in parts])
            tops[u] = top * COEF
            raw[u] = parts

        def soften(u):
            probs[u] = [jnp.exp2(x * COEF - tops[u]).astype(jnp.bfloat16) for x in raw.pop(u)]

        def gather(u):
            h, t = units[u]
            span = pl.ds(t * tile, tile)
            prob = jnp.concatenate(probs.pop(u), axis=0)
            acc_ref[h, :, span] = dot_nn(vt_ref[h // GROUP, :, pl.ds(0, (t + 1) * tile)], prob)
            m_ref[h, :, span] = jnp.broadcast_to(tops[u], (8, tile))

        staged(len(units), scores, soften, gather)

    def finish(h, span, acc):
        ctx_ref[span, head_cols(h)] = (acc[:HD] * (1.0 / acc[HD : HD + 1])).T.astype(jnp.bfloat16)

    units = heads * HALVES - GROUP
    per = PER

    def unit_place(u):
        block = u // GROUP
        g = block // HALVES
        half = lax.rem(block, HALVES)
        keys = pl.ds(pl.multiple_of(half * span_rows, span_rows), span_rows)
        return g, g * GROUP + lax.rem(u, GROUP), keys

    def unit_scores(u, raw, top):
        g, h, keys = unit_place(jnp.minimum(u, units - 1))
        for t in range(2):
            span = pl.ds(t * tile, tile)
            score = dot_nt(ak_ref[keys, head_cols(g)], q_ref[span, head_cols(h)])
            raw[:, span] = score
            high = jnp.max(score, axis=0, keepdims=True) * COEF
            high = jnp.maximum(high, m_ref[h, pl.ds(0, 1), span])
            top[pl.ds(0, 8), span] = jnp.broadcast_to(high, (8, tile))

    def unit_soften(raw, top, prob):
        for t in range(2):
            span = pl.ds(t * tile, tile)
            high = top[pl.ds(0, 1), span]
            prob[:, span] = jnp.exp2(raw[:, span] * COEF - high).astype(jnp.bfloat16)
        top[pl.ds(8, 8), :] = top[pl.ds(0, 8), :]

    def unit_gather(u, prob, top, last):
        g, h, keys = unit_place(jnp.maximum(u, 0))
        slot = jnp.where(u < 0, heads, h)
        for t in range(2):
            span = pl.ds(t * tile, tile)
            high = top[pl.ds(8, 1), span]
            alpha = jnp.exp2(m_ref[slot, pl.ds(0, 1), span] - high)
            acc = dot_nn(avt_ref[g, :, keys], prob[:, span]) + alpha * acc_ref[slot, :, span]
            if last:
                finish(h, span, acc)
            else:
                acc_ref[slot, :, span] = acc
                m_ref[slot, :, span] = jnp.broadcast_to(high, (8, tile))

    def trip(i, last):
        unit_gather(2 * i - 2, prob_a, top_a, last)
        unit_soften(raw_b, top_b, prob_b)
        unit_scores(2 * i, raw_a, top_a)
        unit_gather(2 * i - 1, prob_b, top_b, last)
        unit_soften(raw_a, top_a, prob_a)
        unit_scores(2 * i + 1, raw_b, top_b)

    for copy in place_copies:
        copy.wait()
    length = place_ref[pl.ds(0, 1), :].astype(jnp.float32)
    dest = place_ref[pl.ds(8, 1), :] * CAP + place_ref[pl.ds(16, 1), :]

    def opt_attend(queries, counts, key, value_t):
        size = queries.shape[0]
        stacked = jnp.concatenate([queries[:, j * HD : (j + 1) * HD] for j in range(GROUP)], axis=0)
        score = dot_nt(key, stacked)
        if counts is not None:
            spot = lax.broadcasted_iota(jnp.int32, score.shape, 0).astype(jnp.float32)
            score = jnp.where(spot < counts, score, NEG)
        top = jnp.max(score, axis=0, keepdims=True) * COEF
        acc = dot_nn(value_t, jnp.exp2(score * COEF - top).astype(jnp.bfloat16))
        total = acc[HD : HD + 1]
        part = acc[:HD] * (1.0 / total)
        stat = top * LN2 + jnp.log(total)
        if counts is not None:
            live = counts > 0.0
            part = jnp.where(live, part, 0.0)
            stat = jnp.where(live, stat, NEG)
        part = part.T.astype(jnp.bfloat16)
        stat = jnp.broadcast_to(stat, (HD, stat.shape[1])).T
        return (
            [part[j * size : (j + 1) * size] for j in range(GROUP)],
            [stat[j * size : (j + 1) * size] for j in range(GROUP)],
        )

    step_rows = min(opts, 64)
    lane_opts = GROUP * step_rows

    def options_group(g):
        lanes = lax.broadcasted_iota(jnp.int32, (step_rows, HD), 1)
        for base in range(0, opts, step_rows):
            span = pl.ds(base, step_rows)
            pick = lax.broadcasted_iota(jnp.int32, (opts, lane_opts), 0) - base
            pick = pick == lax.rem(lax.broadcasted_iota(jnp.int32, (opts, lane_opts), 1), step_rows)
            spread = dot_nn(
                jnp.broadcast_to(length, (8, opts)), pick.astype(jnp.float32), lax.Precision.HIGHEST
            )
            counts = jnp.clip(spread[:1] - (me * rows).astype(jnp.float32), 0.0, float(rows))
            queries = oq_ref[span, pl.ds(g * GROUP * HD, GROUP * HD)]
            parts, tops = opt_attend(queries, counts, k_ref[:, pl.ds(g * HD, HD)], vt_ref[g])
            stats = jnp.zeros((step_rows, HD), jnp.float32) if g == 0 else stat_ref[span, :]
            for j in range(GROUP):
                h = g * GROUP + j
                part_ref[span, pl.ds(h * HD, HD)] = parts[j]
                stats = jnp.where(lanes == h, tops[j], stats)
            stat_ref[span, :] = stats

    slots = lax.broadcasted_iota(jnp.int32, (CAP, opts), 0)
    mine = (slots + me * CAP == dest).astype(jnp.float32)
    mine_ref[...] = jnp.broadcast_to(jnp.sum(mine, axis=1, keepdims=True), (CAP, HD))

    def options_scatter():
        for d in range(n):
            hot = (slots + d * CAP == dest).astype(jnp.float32)
            span = pl.ds(d * CAP, CAP)
            pbuf[span, :] = dot_nn(hot.astype(jnp.bfloat16), part_ref[...]).astype(jnp.bfloat16)
            sbuf[span, :] = dot_nn(hot, stat_ref[...], lax.Precision.HIGHEST)

    def down_copies(step):
        to = lax.rem(me - step + n, n)
        span = pl.ds(pl.multiple_of(to * CAP, CAP), CAP)
        return (
            pltpu.make_async_remote_copy(
                src_ref=pbuf.at[span],
                dst_ref=rx_p.at[me],
                send_sem=p_send.at[step - 1],
                recv_sem=p_recv.at[step - 1],
                device_id={"blk": to},
                device_id_type=MESH,
            ),
            pltpu.make_async_remote_copy(
                src_ref=sbuf.at[span],
                dst_ref=rx_s.at[me],
                send_sem=s_send.at[step - 1],
                recv_sem=s_recv.at[step - 1],
                device_id={"blk": to},
                device_id_type=MESH,
            ),
        )

    share = heads // SPLIT

    def up_copies(d, piece, final):
        span = pl.ds(d * CAP, CAP)
        cols = pl.ds(piece * share * HD, share * HD)
        copies = [
            pltpu.make_async_remote_copy(
                src_ref=pbuf.at[span, cols],
                dst_ref=rx_p.at[me, :, cols] if final else up_p.at[d, :, cols],
                send_sem=pu_send.at[d, piece],
                recv_sem=pu_recv.at[d, piece],
                device_id={"blk": up},
                device_id_type=MESH,
            )
        ]
        if piece == 0:
            copies.append(
                pltpu.make_async_remote_copy(
                    src_ref=sbuf.at[span],
                    dst_ref=rx_s.at[me] if final else up_s.at[d],
                    send_sem=su_send.at[d],
                    recv_sem=su_recv.at[d],
                    device_id={"blk": up},
                    device_id_type=MESH,
                )
            )
        return copies

    def send_down():
        for step in range(n - 1, 0, -1):
            @pl.when(me >= step)
            def _():
                for copy in down_copies(step):
                    copy.start()

    def combine(d):
        span = pl.ds(d * CAP, CAP)
        final = me == d - 1
        for piece in range(SPLIT):
            for copy in up_copies(d, piece, False):
                copy.wait_recv()
            if piece == 0:
                low, own_stat = up_s[d], sbuf[span, :]
                top = jnp.maximum(low, own_stat)
                low, own_stat = jnp.exp(low - top), jnp.exp(own_stat - top)
                total = low + own_stat
                sbuf[span, :] = top + jnp.log(total)
                low, own_stat = low / total, own_stat / total
            for h in range(piece * share, (piece + 1) * share):
                cols = pl.ds(h * HD, HD)
                mixed = low[:, h : h + 1] * up_p[d, :, cols].astype(jnp.float32)
                mixed = mixed + own_stat[:, h : h + 1] * pbuf[span, cols].astype(jnp.float32)
                pbuf[span, cols] = mixed.astype(jnp.bfloat16)

            @pl.when(final)
            def _():
                for copy in up_copies(d, piece, True):
                    copy.start()

            @pl.when(jnp.logical_not(final))
            def _():
                for copy in up_copies(d, piece, False):
                    copy.start()

    def send_up_first():
        for d in range(n - 1, 2, -1):
            for piece in range(SPLIT):
                for copy in up_copies(d, piece, False):
                    copy.start()

    def send_up_rest():
        for d in range(n - 1, 2, -1):
            @pl.when(me < d)
            def _():
                combine(d)

    def send_up_last():
        for piece in range(SPLIT):
            for copy in up_copies(hub, piece, True):
                copy.start()

    def options_anchor(g, key_of, value_of):
        hot = mine.astype(jnp.bfloat16)
        lanes = lax.broadcasted_iota(jnp.int32, (CAP, HD), 1)
        queries = dot_nn(hot, oq_ref[:, pl.ds(pl.multiple_of(g * GROUP * HD, GROUP * HD), GROUP * HD)]).astype(jnp.bfloat16)
        parts, tops = opt_attend(queries, None, key_of[:, head_cols(g)], value_of[g])
        stats = rx_s[0]
        for j in range(GROUP):
            h = g * GROUP + j
            rx_p[0, :, head_cols(h)] = parts[j]
            stats = jnp.where(lanes == h, tops[j], stats)
        rx_s[0] = stats

    @pl.when(me == 0)
    def _():
        greet()

    def local_pair(i, carry):
        q_copy(i).wait()
        local_heads([i * PAIR + j for j in range(PAIR)])

        @pl.when((i == GREET) & (me > 0))
        def _():
            greet()

        @pl.when(i == max(pairs - 3, 0))
        def _():
            oq_pass(1)

        @pl.when((i >= pairs - 2) & (me == 1) & (me < n - 1))
        def _():
            forward(i - (pairs - 2))

        return carry

    lax.fori_loop(0, pairs, local_pair, 0)

    relay_down = (me == hub) & (me > 1)
    relay_up = (me >= hub) & (me < n - 1)

    def oq_wait():
        o_copy.wait()

        @pl.when(me > 0)
        def _():
            oq_first(0, up, True).wait_recv()

        @pl.when(relay_up)
        def _():
            oq_first(0, up, True).start()

        @pl.when(relay_down)
        def _():
            oq_first(1, below, True).start()

        for step in range(2, n - 1):
            oq_pass(step)
        for step in range(1, n):
            @pl.when(me + step < n)
            def _():
                oq_copy(step).wait_recv()

    @pl.when(me == 0)
    def _():
        oq_wait()

        def whole(h, carry):
            for t in range(2):
                span = pl.ds(t * tile, tile)
                finish(h, span, acc_ref[h, :, span])
            return carry

        lax.fori_loop(0, heads, whole, 0)
        rx_s[0] = jnp.zeros_like(rx_s[0])
        for g in range(kvs):
            options_anchor(g, k_ref, vt_ref)

    @pl.when(me > 0)
    def _():

        def forward_range(low, high):
            def one(c, carry):
                forward(c)
                return carry

            lax.fori_loop(low, high, one, 0)

        @pl.when(me == 1)
        def _():
            forward_range(jnp.where(me < n - 1, 2, 0), PIECES)

        steps = units // 2 + 1
        early = min(PER + 1, steps - 1)
        sent = min(early + PIECES, steps - 1)

        def forward_early(c):
            @pl.when((me == 1) & (c < chunks))
            def _():
                forward(c)

        def options_all():
            oq_wait()
            for g in range(kvs):
                options_group(g)
                forward_early(PIECES + early + g)
            options_scatter()
            forward_early(PIECES + early + kvs)
            send_down()
            own_slots = pl.ds(pl.multiple_of(me * CAP, CAP), CAP)
            rx_p[me] = pbuf[own_slots, :]
            rx_s[me] = sbuf[own_slots, :]
            for b in range(1, n - 2):
                @pl.when(b < me - 1)
                def _():
                    rx_p[b] = jnp.zeros_like(rx_p[b])
                    rx_s[b] = jnp.full_like(rx_s[b], NEG)


            @pl.when(me > 1)
            def _():
                forward_range(0, PIECES)

        turn = jnp.where(me == 1, early, 0)
        rx_s[0] = jnp.zeros_like(rx_s[0])

        def turn_values(u):
            g, _, keys = unit_place(u)
            avt_ref[g, :HD, keys] = av_ref[keys, head_cols(g)].T

        def anchor_step(i, carry):
            @pl.when(i == turn)
            def _():
                options_all()

            @pl.when((lax.rem(i, per) == 0) & (2 * i < units))
            def _():
                turn_values(2 * i)

            last = lax.rem((jnp.maximum(i, 1) - 1) // per, HALVES) == HALVES - 1

            @pl.when(last)
            def _():
                trip(i, True)

            @pl.when(jnp.logical_not(last))
            def _():
                trip(i, False)

            following = PIECES + i + jnp.where((me == 1) & (i >= early), kvs + 1, 0)

            @pl.when(following < chunks)
            def _():
                forward(following)

            @pl.when((me == 1) & (i == sent))
            def _():
                send_up_first()

            @pl.when((lax.rem(i, per * HALVES) == 0) & (i > 0) & (me == n - 1))
            def _():
                options_anchor(i // (per * HALVES) - 1, ak_ref, avt_ref)

            return carry

        lax.fori_loop(0, steps, anchor_step, 0)

        turn_values(units)

        @pl.when((me == 1) & (me < n - 1))
        def _():
            send_up_last()

        @pl.when((me > 1) & (me < n - 1))
        def _():
            send_up_rest()

        def options_rest(g, carry):
            options_anchor(g, ak_ref, avt_ref)
            return carry

        lax.fori_loop(jnp.where(me < n - 1, 0, kvs - 1), kvs, options_rest, 0)

    for step in range(1, n):
        @pl.when(me + step < n)
        def _():
            for copy in down_copies(step):
                copy.wait_recv()

    for d in range(2, n):
        @pl.when(me == d)
        def _():
            for piece in range(SPLIT):
                for copy in up_copies(d, piece, True):
                    copy.wait_recv()

    for step in range(1, n):
        @pl.when(me >= step)
        def _():
            oq_copy(step).wait_send()

        @pl.when((me >= step) & (me < n - 1))
        def _():
            oq_up(step).wait_send()

    @pl.when((me == 0) | relay_up)
    def _():
        oq_first(0, up, True).wait_send()

    @pl.when(relay_down)
    def _():
        oq_first(1, below, True).wait_send()

    @pl.when(me == 0)
    def _():
        def drain(c, carry):
            for copy in anchor_copies(c, True):
                copy.wait_send()
            return carry

        lax.fori_loop(0, chunks, drain, 0)

    @pl.when((me > 0) & (me < n - 1))
    def _():
        def drain(c, carry):
            for copy in anchor_copies(c, False):
                copy.wait_send()
            return carry

        lax.fori_loop(0, chunks, drain, 0)

    for step in range(1, n):
        @pl.when(me >= step)
        def _():
            for copy in down_copies(step):
                copy.wait_send()

    for d in range(2, n):
        @pl.when((me > 0) & (me < d))
        def _():
            for piece in range(SPLIT):
                for copy in up_copies(d, piece, False):
                    copy.wait_send()


def merge(
    n,
    ctx_ref, rx_p, rx_s, mine_ref, q_ref, ak_ref, avt_ref, acc_ref, m_ref,
    ctx_hbm, opt_ref,
    tail_ref, sem, tail_sem,
):
    me = lax.axis_index("blk")
    rows, width = ctx_ref.shape
    heads = width // HD
    tile = rows // 2
    base = heads - GROUP
    g = base // GROUP
    span_rows = rows // HALVES
    keys = pl.ds((HALVES - 1) * span_rows, span_rows)
    part = rows // WRITES

    def early_copies():
        return [
            pltpu.make_async_copy(
                ctx_ref.at[pl.ds(i * part, part), pl.ds(0, base * HD)],
                ctx_hbm.at[pl.ds(i * part, part), pl.ds(0, base * HD)],
                sem.at[i],
            )
            for i in range(WRITES)
        ]

    def tail_copy(i, src):
        cols = pl.ds(i * PAIR * HD, PAIR * HD)
        return pltpu.make_async_copy(
            src.at[:, cols if src is tail_ref else pl.ds((base + i * PAIR) * HD, PAIR * HD)],
            ctx_hbm.at[:, pl.ds((base + i * PAIR) * HD, PAIR * HD)],
            tail_sem.at[i],
        )

    if base:
        for copy in early_copies():
            copy.start()

    top = rx_s[0]
    for b in range(1, n):
        top = jnp.maximum(top, rx_s[b])
    weights = [jnp.exp(rx_s[b] - top) for b in range(n)]
    scale = 1.0 / functools.reduce(jnp.add, weights)
    weights = [x * scale for x in weights]
    occupied = mine_ref[...] > 0.0

    def merge_head(h):
        cols = pl.ds(h * HD, HD)
        merged = jnp.zeros((CAP, HD), jnp.float32)
        for b in range(n):
            merged = merged + weights[b][:, h : h + 1] * rx_p[b, :, cols].astype(jnp.float32)
        opt_ref[:, cols] = jnp.where(occupied, merged, 0.0).astype(jnp.bfloat16)

    @pl.when(me == 0)
    def _():
        for i in range(GROUP // PAIR):
            tail_copy(i, ctx_ref).start()
        for h in range(heads):
            merge_head(h)

    @pl.when(me > 0)
    def _():
        units = [(j, t) for j in range(GROUP) for t in range(2)]
        raw, tops, probs = {}, {}, {}

        def scores(u):
            j, t = units[u]
            span = pl.ds(t * tile, tile)
            query = q_ref[span, pl.ds((base + j) * HD, HD)]
            raw[u] = dot_nt(ak_ref[keys, pl.ds(g * HD, HD)], query)
            high = jnp.max(raw[u], axis=0, keepdims=True) * COEF
            tops[u] = jnp.maximum(high, m_ref[base + j, pl.ds(0, 1), span])

        def soften(u):
            probs[u] = jnp.exp2(raw.pop(u) * COEF - tops[u]).astype(jnp.bfloat16)

        def gather(u):
            j, t = units[u]
            span = pl.ds(t * tile, tile)
            alpha = jnp.exp2(m_ref[base + j, pl.ds(0, 1), span] - tops[u])
            acc = dot_nn(avt_ref[g, :, keys], probs.pop(u)) + alpha * acc_ref[base + j, :, span]
            out = (acc[:HD] * (1.0 / acc[HD : HD + 1])).T.astype(jnp.bfloat16)
            tail_ref[span, pl.ds(j * HD, HD)] = out
            for h in range(u * heads // len(units), (u + 1) * heads // len(units)):
                merge_head(h)
            if t == 1 and j % PAIR == PAIR - 1:
                tail_copy(j // PAIR, tail_ref).start()

        staged(len(units), scores, soften, gather)

    if base:
        for copy in early_copies():
            copy.wait()
    for i in range(GROUP // PAIR):
        tail_copy(i, ctx_ref).wait()


def body(ctx_query, ctx_key, ctx_value, opt_query, opt_owner, opt_slot, opt_length):
    n = lax.axis_size("blk")
    rows, width = ctx_query.shape
    heads = width // HD
    kvs = ctx_key.shape[1] // HD
    opts = opt_length.shape[0]
    chunks = HALVES * PIECES * kvs
    bf16, f32 = jnp.bfloat16, jnp.float32
    dma = pltpu.SemaphoreType.DMA
    hbm = pl.BlockSpec(memory_space=pltpu.HBM)
    vmem = pl.BlockSpec(memory_space=pltpu.VMEM)
    length, owner, slot = (x.reshape(1, opts) for x in (opt_length, opt_owner, opt_slot))
    kept = 2 * width * (2 * rows + n * CAP) + 4 * HD * CAP * (n + 1)
    kept += 2 * rows * kvs * (HD + VR) + 4 * (heads + 1) * (VR + 8) * rows
    state = pl.pallas_call(
        functools.partial(attend, n),
        out_shape=(
            pltpu.VMEM((rows, width), bf16),
            pltpu.VMEM((n, CAP, width), bf16),
            pltpu.VMEM((n, CAP, HD), f32),
            pltpu.VMEM((CAP, HD), f32),
            pltpu.VMEM((rows, width), bf16),
            pltpu.VMEM((rows, kvs * HD), bf16),
            pltpu.VMEM((kvs, VR, rows), bf16),
            pltpu.VMEM((heads + 1, VR, rows), f32),
            pltpu.VMEM((heads + 1, 8, rows), f32),
        ),
        in_specs=[hbm] * 7,
        out_specs=(vmem,) * 9,
        scratch_shapes=[
            pltpu.VMEM((rows, kvs * HD), bf16),
            pltpu.VMEM((rows, kvs * HD), bf16),
            pltpu.VMEM((kvs, VR, rows), bf16),
            pltpu.VMEM((rows, kvs * HD), bf16),
            pltpu.VMEM((opts, width), bf16),
            pltpu.VMEM((rows // HALVES, rows), f32),
            pltpu.VMEM((rows // HALVES, rows), f32),
            pltpu.VMEM((rows // HALVES, rows), bf16),
            pltpu.VMEM((rows // HALVES, rows), bf16),
            pltpu.VMEM((16, rows), f32),
            pltpu.VMEM((16, rows), f32),
            pltpu.VMEM((opts, width), bf16),
            pltpu.VMEM((opts, HD), f32),
            pltpu.VMEM((n * CAP, width), bf16),
            pltpu.VMEM((n * CAP, HD), f32),
            pltpu.VMEM((n, CAP, width), bf16),
            pltpu.VMEM((n, CAP, HD), f32),
            pltpu.VMEM((24, opts), jnp.int32),
            dma((3,)), dma((heads // PAIR,)), dma(()), dma(()), dma(()),
            dma((n - 1,)), dma((n - 1,)), dma((n - 1,)), dma((n - 1,)), dma((2,)), dma(()),
            dma((chunks,)), dma((chunks,)), dma((chunks,)), dma((chunks,)),
            dma((n - 1,)), dma((n - 1,)), dma((n - 1,)), dma((n - 1,)),
            dma((n, SPLIT)), dma((n, SPLIT)), dma((n,)), dma((n,)),
            pltpu.SemaphoreType.REGULAR, pltpu.SemaphoreType.REGULAR,
        ],
        compiler_params=pltpu.CompilerParams(
            collective_id=0, has_side_effects=True, vmem_limit_bytes=LIMIT - kept
        ),
        name="star",
    )(ctx_query, ctx_key, ctx_value, opt_query, length, owner, slot)
    return pl.pallas_call(
        functools.partial(merge, n),
        out_shape=(
            jax.ShapeDtypeStruct((rows, width), bf16),
            jax.ShapeDtypeStruct((CAP, width), bf16),
        ),
        in_specs=[vmem] * 9,
        out_specs=(hbm, vmem),
        scratch_shapes=[
            pltpu.VMEM((rows, GROUP * HD), bf16),
            dma((WRITES,)),
            dma((GROUP // PAIR,)),
        ],
        compiler_params=pltpu.CompilerParams(vmem_limit_bytes=16 * 1024 * 1024),
        name="merge",
    )(*state)


def solution(mesh):
    return jax.shard_map(
        body,
        mesh=mesh,
        in_specs=(
            P(("groups", "blk"), "head"),
            P(("groups", "blk"), "head"),
            P(("groups", "blk"), "head"),
            P(("groups", "blk"), "head"),
            P("groups"),
            P("groups"),
            P("groups"),
        ),
        out_specs=(P(("groups", "blk"), "head"), P(("groups", "blk"), "head")),
        check_vma=False,
    )
```

```python
import functools
import math

import jax
import jax.numpy as jnp
from jax import lax
from jax.experimental import pallas as pl
from jax.experimental.pallas import tpu as pltpu
from jax.sharding import PartitionSpec as P

HD = 128
HQ = 64
KVH = 8
CAP = 32
GROUP = HQ // KVH
MESH = pl.DeviceIdType.MESH
NEG = -1e30
LN2 = math.log(2.0)
COEF = HD**-0.5 / LN2
PAIR = 2
HALVES = 2
PIECES = 4
VR = HD + 16
PER = GROUP // 2
WRITES = 8
LEAD = 2
SPLIT = 2
TAIL = 6
LIMIT = 65100 * 1024
GREET = 0


def dot_nt(a, b):
    return lax.dot_general(a, b, (((1,), (1,)), ((), ())), preferred_element_type=jnp.float32)


def dot_nn(a, b, precision=None):
    return lax.dot_general(
        a, b, (((1,), (0,)), ((), ())), preferred_element_type=jnp.float32, precision=precision
    )


def staged(count, scores, soften, gather):
    for k in range(count + 2):
        if k < count:
            scores(k)
        if 0 <= k - 1 < count:
            soften(k - 1)
        if 0 <= k - 2 < count:
            gather(k - 2)


def attend(
    n,
    q_hbm, k_hbm, v_hbm, oq_hbm, len_hbm, owner_hbm, slot_hbm,
    ctx_ref, rx_p, rx_s, mine_ref, q_ref, ak_ref, avt_ref, acc_ref, m_ref,
    k_ref, v_ref, vt_ref, oq_ref,
    raw_a, raw_b, prob_a, prob_b, top_a, top_b, part_ref, stat_ref, pbuf, sbuf, up_p, up_s, place_ref,
    place_sem, q_sem, k_sem, v_sem, o_sem,
    oq_send, oq_recv, ou_send, ou_recv, oz_send, oz_recv, ak_send, ak_recv, av_send,
    p_send, p_recv, s_send, s_recv, pu_send, pu_recv, su_send, su_recv, low_sem, near_sem,
):
    me = lax.axis_index("blk")
    rows = q_ref.shape[0]
    heads = q_ref.shape[1] // HD
    kvs = k_ref.shape[1] // HD
    entry = oq_hbm.shape[0]
    opts = oq_ref.shape[0]
    pairs = heads // PAIR
    tile = rows // 2
    span_rows = rows // HALVES
    chunk = span_rows // PIECES
    chunks = kvs * HALVES * PIECES

    def q_copy(i):
        cols = pl.ds(pl.multiple_of(i * PAIR * HD, PAIR * HD), PAIR * HD)
        return pltpu.make_async_copy(q_hbm.at[:, cols], q_ref.at[:, cols], q_sem.at[i])

    k_copy = pltpu.make_async_copy(k_hbm, k_ref, k_sem)
    v_copy = pltpu.make_async_copy(v_hbm, v_ref, v_sem)
    own = pl.ds(pl.multiple_of(me * entry, entry), entry)
    o_copy = pltpu.make_async_copy(oq_hbm, oq_ref.at[own], o_sem)

    place_copies = [
        pltpu.make_async_copy(src, place_ref.at[pl.ds(8 * i, 1)], place_sem.at[i])
        for i, src in enumerate((len_hbm, owner_hbm, slot_hbm))
    ]
    barrier = pltpu.get_barrier_semaphore()
    up = lax.rem(me + 1, n)
    below = lax.rem(me - 1 + n, n)

    @pl.when(me < n - 1)
    def _():
        pl.semaphore_signal(barrier, inc=1, device_id={"blk": up}, device_id_type=MESH)

    @pl.when(me > 0)
    def _():
        pl.semaphore_signal(barrier, inc=1, device_id={"blk": below}, device_id_type=MESH)

    k_copy.start()
    q_copy(0).start()
    v_copy.start()
    for i in range(1, pairs):
        q_copy(i).start()
    o_copy.start()
    for copy in place_copies:
        copy.start()

    def oq_copy(step):
        return pltpu.make_async_remote_copy(
            src_ref=oq_hbm,
            dst_ref=oq_ref.at[own],
            send_sem=oq_send.at[step - 1],
            recv_sem=oq_recv.at[step - 1],
            device_id={"blk": lax.rem(me - step + n, n)},
            device_id_type=MESH,
        )

    def oq_up(step):
        at = lax.rem(me + 1 - step + n, n)
        span = pl.ds(pl.multiple_of(at * entry, entry), entry)
        return pltpu.make_async_remote_copy(
            src_ref=oq_hbm if step == 1 else oq_ref.at[span],
            dst_ref=oq_ref.at[span],
            send_sem=ou_send.at[step - 1],
            recv_sem=ou_recv.at[step - 1],
            device_id={"blk": up},
            device_id_type=MESH,
        )

    def oq_pass(step):
        @pl.when(me > step)
        def _():
            oq_up(step).wait_recv()

        @pl.when((me > step) & (me < n - 1))
        def _():
            oq_up(step + 1).start()

    first_rows = pl.ds(0, entry)

    hub = min(2, n - 1)

    def oq_first(index, to, relay):
        return pltpu.make_async_remote_copy(
            src_ref=oq_ref.at[first_rows] if relay else oq_hbm,
            dst_ref=oq_ref.at[first_rows],
            send_sem=oz_send.at[index],
            recv_sem=oz_recv,
            device_id={"blk": to},
            device_id_type=MESH,
        )

    def head_cols(h):
        return pl.ds(pl.multiple_of(h * HD, HD), HD)

    def anchor_copies(c, first):
        g = c // (HALVES * PIECES)
        r = lax.rem(c, HALVES * PIECES)
        span = pl.ds(pl.multiple_of(r * chunk, chunk), chunk)

        def copy(src, cols, send):
            return pltpu.make_async_remote_copy(
                src_ref=src,
                dst_ref=ak_ref.at[span, cols],
                send_sem=send.at[c],
                recv_sem=ak_recv.at[c],
                device_id={"blk": up},
                device_id_type=MESH,
            )

        if not first:
            both = pl.ds(pl.multiple_of(2 * g * HD, 2 * HD), 2 * HD)
            return (copy(ak_ref.at[span, both], both, ak_send),)
        return (
            copy(k_hbm.at[span, head_cols(g)], head_cols(2 * g), ak_send),
            copy(v_hbm.at[span, head_cols(g)], head_cols(2 * g + 1), av_send),
        )

    def send_anchor(low, high):
        def send(c, carry):
            for copy in anchor_copies(c, True):
                copy.start()
            return carry

        lax.fori_loop(low, high, send, 0)

    def greet():
        @pl.when((me > 0) & (me < n - 1))
        def _():
            pl.semaphore_wait(barrier, 2)

        @pl.when((me == 0) | (me == n - 1))
        def _():
            pl.semaphore_wait(barrier, 1)

        @pl.when(me == 0)
        def _():
            send_anchor(0, LEAD)

        @pl.when(me > 1)
        def _():
            pl.semaphore_wait(low_sem, 1)

        @pl.when((me > 0) & (me < n - 1))
        def _():
            pl.semaphore_signal(low_sem, inc=1, device_id={"blk": up}, device_id_type=MESH)

        @pl.when((me == 1) & (me < n - 1))
        def _():
            pl.semaphore_signal(near_sem, inc=1, device_id={"blk": below}, device_id_type=MESH)

        if n > 2:
            @pl.when(me == 0)
            def _():
                pl.semaphore_wait(near_sem, 1)

        @pl.when(me == 0)
        def _():
            oq_first(0, hub, False).start()
            send_anchor(LEAD, chunks)

        @pl.when((me > 0) & (me < n - 1))
        def _():
            oq_up(1).start()

        for step in range(1, n):
            @pl.when(me >= step)
            def _():
                oq_copy(step).start()

    def forward(c):
        for copy in anchor_copies(c, False):
            copy.wait_recv()

        @pl.when(me < n - 1)
        def _():
            for copy in anchor_copies(c, False):
                copy.start()

    ones = jnp.ones((VR - HD, rows), jnp.bfloat16)
    k_copy.wait()
    v_copy.wait()
    for g in range(kvs):
        vt_ref[g, :HD, :] = v_ref[:, g * HD : (g + 1) * HD].T
        vt_ref[g, HD:, :] = ones
        avt_ref[g, HD:, :] = ones

    causal = lax.broadcasted_iota(jnp.int32, (tile, tile), 0) <= lax.broadcasted_iota(
        jnp.int32, (tile, tile), 1
    )

    def local_heads(hs):
        units = [(h, t) for h in hs for t in range(2)]
        raw, tops, probs = {}, {}, {}

        def scores(u):
            h, t = units[u]
            query = q_ref[pl.ds(t * tile, tile), head_cols(h)]
            score = dot_nt(k_ref[pl.ds(0, (t + 1) * tile), head_cols(h // GROUP)], query)
            parts = [score[j * tile : (j + 1) * tile] for j in range(t + 1)]
            parts[t] = jnp.where(causal, parts[t], NEG)
            top = functools.reduce(jnp.maximum, [jnp.max(x, axis=0, keepdims=True) for x in parts])
            tops[u] = top * COEF
            raw[u] = parts

        def soften(u):
            probs[u] = [jnp.exp2(x * COEF - tops[u]).astype(jnp.bfloat16) for x in raw.pop(u)]

        def gather(u):
            h, t = units[u]
            span = pl.ds(t * tile, tile)
            prob = jnp.concatenate(probs.pop(u), axis=0)
            acc_ref[h, :, span] = dot_nn(vt_ref[h // GROUP, :, pl.ds(0, (t + 1) * tile)], prob)
            m_ref[h, :, span] = jnp.broadcast_to(tops[u], (8, tile))

        staged(len(units), scores, soften, gather)

    def finish(h, span, acc):
        ctx_ref[span, head_cols(h)] = (acc[:HD] * (1.0 / acc[HD : HD + 1])).T.astype(jnp.bfloat16)

    units = heads * HALVES - TAIL
    per = PER

    def unit_place(u):
        block = u // GROUP
        g = block // HALVES
        half = lax.rem(block, HALVES)
        keys = pl.ds(pl.multiple_of(half * span_rows, span_rows), span_rows)
        return g, g * GROUP + lax.rem(u, GROUP), keys

    def unit_scores(u, raw, top):
        g, h, keys = unit_place(jnp.minimum(u, units - 1))
        for t in range(2):
            span = pl.ds(t * tile, tile)
            score = dot_nt(ak_ref[keys, head_cols(2 * g)], q_ref[span, head_cols(h)])
            raw[:, span] = score
            high = jnp.max(score, axis=0, keepdims=True) * COEF
            high = jnp.maximum(high, m_ref[h, pl.ds(0, 1), span])
            top[pl.ds(0, 8), span] = jnp.broadcast_to(high, (8, tile))

    def unit_soften(raw, top, prob):
        for t in range(2):
            span = pl.ds(t * tile, tile)
            high = top[pl.ds(0, 1), span]
            prob[:, span] = jnp.exp2(raw[:, span] * COEF - high).astype(jnp.bfloat16)
        top[pl.ds(8, 8), :] = top[pl.ds(0, 8), :]

    def unit_gather(u, prob, top, last):
        g, h, keys = unit_place(jnp.maximum(u, 0))
        slot = jnp.where(u < 0, heads, h)
        for t in range(2):
            span = pl.ds(t * tile, tile)
            high = top[pl.ds(8, 1), span]
            alpha = jnp.exp2(m_ref[slot, pl.ds(0, 1), span] - high)
            acc = dot_nn(avt_ref[g, :, keys], prob[:, span]) + alpha * acc_ref[slot, :, span]
            if last:
                finish(h, span, acc)
            else:
                acc_ref[slot, :, span] = acc
                m_ref[slot, :, span] = jnp.broadcast_to(high, (8, tile))

    def trip(i, last):
        unit_gather(2 * i - 2, prob_a, top_a, last)
        unit_soften(raw_b, top_b, prob_b)
        unit_scores(2 * i, raw_a, top_a)
        unit_gather(2 * i - 1, prob_b, top_b, last)
        unit_soften(raw_a, top_a, prob_a)
        unit_scores(2 * i + 1, raw_b, top_b)

    for copy in place_copies:
        copy.wait()
    length = place_ref[pl.ds(0, 1), :].astype(jnp.float32)
    dest = place_ref[pl.ds(8, 1), :] * CAP + place_ref[pl.ds(16, 1), :]

    def opt_attend(queries, counts, key, value_t):
        size = queries.shape[0]
        stacked = jnp.concatenate([queries[:, j * HD : (j + 1) * HD] for j in range(GROUP)], axis=0)
        score = dot_nt(key, stacked)
        if counts is not None:
            spot = lax.broadcasted_iota(jnp.int32, score.shape, 0).astype(jnp.float32)
            score = jnp.where(spot < counts, score, NEG)
        top = jnp.max(score, axis=0, keepdims=True) * COEF
        acc = dot_nn(value_t, jnp.exp2(score * COEF - top).astype(jnp.bfloat16))
        total = acc[HD : HD + 1]
        part = acc[:HD] * (1.0 / total)
        stat = top * LN2 + jnp.log(total)
        if counts is not None:
            live = counts > 0.0
            part = jnp.where(live, part, 0.0)
            stat = jnp.where(live, stat, NEG)
        part = part.T.astype(jnp.bfloat16)
        stat = jnp.broadcast_to(stat, (HD, stat.shape[1])).T
        return (
            [part[j * size : (j + 1) * size] for j in range(GROUP)],
            [stat[j * size : (j + 1) * size] for j in range(GROUP)],
        )

    step_rows = min(opts, 64)
    lane_opts = GROUP * step_rows

    def options_group(g):
        lanes = lax.broadcasted_iota(jnp.int32, (step_rows, HD), 1)
        for base in range(0, opts, step_rows):
            span = pl.ds(base, step_rows)
            pick = lax.broadcasted_iota(jnp.int32, (opts, lane_opts), 0) - base
            pick = pick == lax.rem(lax.broadcasted_iota(jnp.int32, (opts, lane_opts), 1), step_rows)
            spread = dot_nn(
                jnp.broadcast_to(length, (8, opts)), pick.astype(jnp.float32), lax.Precision.HIGHEST
            )
            counts = jnp.clip(spread[:1] - (me * rows).astype(jnp.float32), 0.0, float(rows))
            queries = oq_ref[span, pl.ds(g * GROUP * HD, GROUP * HD)]
            parts, tops = opt_attend(queries, counts, k_ref[:, pl.ds(g * HD, HD)], vt_ref[g])
            stats = jnp.zeros((step_rows, HD), jnp.float32) if g == 0 else stat_ref[span, :]
            for j in range(GROUP):
                h = g * GROUP + j
                part_ref[span, pl.ds(h * HD, HD)] = parts[j]
                stats = jnp.where(lanes == h, tops[j], stats)
            stat_ref[span, :] = stats

    slots = lax.broadcasted_iota(jnp.int32, (CAP, opts), 0)
    mine = (slots + me * CAP == dest).astype(jnp.float32)
    mine_ref[...] = jnp.broadcast_to(jnp.sum(mine, axis=1, keepdims=True), (CAP, HD))

    def options_scatter():
        for d in range(n):
            hot = (slots + d * CAP == dest).astype(jnp.float32)
            span = pl.ds(d * CAP, CAP)
            pbuf[span, :] = dot_nn(hot.astype(jnp.bfloat16), part_ref[...]).astype(jnp.bfloat16)
            sbuf[span, :] = dot_nn(hot, stat_ref[...], lax.Precision.HIGHEST)

    def down_copies(step):
        to = lax.rem(me - step + n, n)
        span = pl.ds(pl.multiple_of(to * CAP, CAP), CAP)
        return (
            pltpu.make_async_remote_copy(
                src_ref=pbuf.at[span],
                dst_ref=rx_p.at[me],
                send_sem=p_send.at[step - 1],
                recv_sem=p_recv.at[step - 1],
                device_id={"blk": to},
                device_id_type=MESH,
            ),
            pltpu.make_async_remote_copy(
                src_ref=sbuf.at[span],
                dst_ref=rx_s.at[me],
                send_sem=s_send.at[step - 1],
                recv_sem=s_recv.at[step - 1],
                device_id={"blk": to},
                device_id_type=MESH,
            ),
        )

    share = heads // SPLIT

    def up_copies(d, piece, final):
        span = pl.ds(d * CAP, CAP)
        cols = pl.ds(piece * share * HD, share * HD)
        copies = [
            pltpu.make_async_remote_copy(
                src_ref=pbuf.at[span, cols],
                dst_ref=rx_p.at[me, :, cols] if final else up_p.at[d, :, cols],
                send_sem=pu_send.at[d, piece],
                recv_sem=pu_recv.at[d, piece],
                device_id={"blk": up},
                device_id_type=MESH,
            )
        ]
        if piece == 0:
            copies.append(
                pltpu.make_async_remote_copy(
                    src_ref=sbuf.at[span],
                    dst_ref=rx_s.at[me] if final else up_s.at[d],
                    send_sem=su_send.at[d],
                    recv_sem=su_recv.at[d],
                    device_id={"blk": up},
                    device_id_type=MESH,
                )
            )
        return copies

    def send_down():
        for step in range(n - 1, 0, -1):
            @pl.when(me >= step)
            def _():
                for copy in down_copies(step):
                    copy.start()

    def combine(d):
        span = pl.ds(d * CAP, CAP)
        final = me == d - 1
        for piece in range(SPLIT):
            for copy in up_copies(d, piece, False):
                copy.wait_recv()
            if piece == 0:
                low, own_stat = up_s[d], sbuf[span, :]
                top = jnp.maximum(low, own_stat)
                low, own_stat = jnp.exp(low - top), jnp.exp(own_stat - top)
                total = low + own_stat
                sbuf[span, :] = top + jnp.log(total)
                low, own_stat = low / total, own_stat / total
            for h in range(piece * share, (piece + 1) * share):
                cols = pl.ds(h * HD, HD)
                mixed = low[:, h : h + 1] * up_p[d, :, cols].astype(jnp.float32)
                mixed = mixed + own_stat[:, h : h + 1] * pbuf[span, cols].astype(jnp.float32)
                pbuf[span, cols] = mixed.astype(jnp.bfloat16)

            @pl.when(final)
            def _():
                for copy in up_copies(d, piece, True):
                    copy.start()

            @pl.when(jnp.logical_not(final))
            def _():
                for copy in up_copies(d, piece, False):
                    copy.start()

    def send_up_first():
        for d in range(n - 1, 2, -1):
            for piece in range(SPLIT):
                for copy in up_copies(d, piece, False):
                    copy.start()

    def send_up_rest():
        for d in range(n - 1, 2, -1):
            @pl.when(me < d)
            def _():
                combine(d)

    def send_up_last():
        for piece in range(SPLIT):
            for copy in up_copies(hub, piece, True):
                copy.start()

    def options_anchor(g, key_of, value_of, stride):
        hot = mine.astype(jnp.bfloat16)
        lanes = lax.broadcasted_iota(jnp.int32, (CAP, HD), 1)
        queries = dot_nn(hot, oq_ref[:, pl.ds(pl.multiple_of(g * GROUP * HD, GROUP * HD), GROUP * HD)]).astype(jnp.bfloat16)
        parts, tops = opt_attend(queries, None, key_of[:, head_cols(stride * g)], value_of[g])
        stats = rx_s[0]
        for j in range(GROUP):
            h = g * GROUP + j
            rx_p[0, :, head_cols(h)] = parts[j]
            stats = jnp.where(lanes == h, tops[j], stats)
        rx_s[0] = stats

    @pl.when(me == 0)
    def _():
        greet()

    def local_pair(i, carry):
        q_copy(i).wait()
        local_heads([i * PAIR + j for j in range(PAIR)])

        @pl.when((i == GREET) & (me > 0))
        def _():
            greet()

        @pl.when(i == max(pairs - 3, 0))
        def _():
            oq_pass(1)

        @pl.when((i >= pairs - 2) & (me == 1) & (me < n - 1))
        def _():
            forward(i - (pairs - 2))

        return carry

    lax.fori_loop(0, pairs, local_pair, 0)

    relay_down = (me == hub) & (me > 1)
    relay_up = (me >= hub) & (me < n - 1)

    def oq_wait():
        o_copy.wait()

        @pl.when(me > 0)
        def _():
            oq_first(0, up, True).wait_recv()

        @pl.when(relay_up)
        def _():
            oq_first(0, up, True).start()

        @pl.when(relay_down)
        def _():
            oq_first(1, below, True).start()

        for step in range(2, n - 1):
            oq_pass(step)
        for step in range(1, n):
            @pl.when(me + step < n)
            def _():
                oq_copy(step).wait_recv()

    @pl.when(me == 0)
    def _():
        oq_wait()

        def whole(h, carry):
            for t in range(2):
                span = pl.ds(t * tile, tile)
                finish(h, span, acc_ref[h, :, span])
            return carry

        lax.fori_loop(0, heads, whole, 0)
        rx_s[0] = jnp.zeros_like(rx_s[0])
        for g in range(kvs):
            options_anchor(g, k_ref, vt_ref, 1)

    @pl.when(me > 0)
    def _():

        def forward_range(low, high):
            def one(c, carry):
                forward(c)
                return carry

            lax.fori_loop(low, high, one, 0)

        @pl.when(me == 1)
        def _():
            forward_range(jnp.where(me < n - 1, 2, 0), PIECES)

        steps = units // 2 + 1
        early = min(PER + 1, steps - 1)
        sent = min(early + PIECES, steps - 1)
        closing = min(chunks - PIECES, steps - 1)

        def forward_early(c):
            @pl.when((me == 1) & (c < chunks))
            def _():
                forward(c)

        def options_all():
            oq_wait()
            for g in range(kvs):
                options_group(g)
                forward_early(PIECES + early + g)
            options_scatter()
            forward_early(PIECES + early + kvs)
            send_down()
            own_slots = pl.ds(pl.multiple_of(me * CAP, CAP), CAP)
            rx_p[me] = pbuf[own_slots, :]
            rx_s[me] = sbuf[own_slots, :]
            for b in range(1, n - 2):
                @pl.when(b < me - 1)
                def _():
                    rx_p[b] = jnp.zeros_like(rx_p[b])
                    rx_s[b] = jnp.full_like(rx_s[b], NEG)


            @pl.when(me > 1)
            def _():
                forward_range(0, PIECES)

        turn = jnp.where(me == 1, early, 0)
        rx_s[0] = jnp.zeros_like(rx_s[0])

        def turn_values(u):
            g, _, keys = unit_place(u)
            avt_ref[g, :HD, keys] = ak_ref[keys, head_cols(2 * g + 1)].T

        def anchor_step(i, carry):
            @pl.when(i == turn)
            def _():
                options_all()

            @pl.when((lax.rem(i, per) == 0) & (2 * i < units))
            def _():
                turn_values(2 * i)

            last = lax.rem((jnp.maximum(i, 1) - 1) // per, HALVES) == HALVES - 1

            @pl.when(last)
            def _():
                trip(i, True)

            @pl.when(jnp.logical_not(last))
            def _():
                trip(i, False)

            following = PIECES + i + jnp.where((me == 1) & (i >= early), kvs + 1, 0)

            @pl.when(following < chunks)
            def _():
                forward(following)

            @pl.when((me == 1) & (i == sent))
            def _():
                send_up_first()

            @pl.when((me == 1) & (me < n - 1) & (i == max(closing, sent)))
            def _():
                send_up_last()

            @pl.when((me > 1) & (me < n - 1) & (i == closing))
            def _():
                send_up_rest()

            @pl.when((lax.rem(i, per * HALVES) == per + 1) & (me == n - 1))
            def _():
                options_anchor(i // (per * HALVES), ak_ref, avt_ref, 2)

            return carry

        lax.fori_loop(0, steps, anchor_step, 0)

        def options_rest(g, carry):
            options_anchor(g, ak_ref, avt_ref, 2)
            return carry

        @pl.when(me < n - 1)
        def _():
            lax.fori_loop(0, kvs, options_rest, 0)

    for step in range(1, n):
        @pl.when(me + step < n)
        def _():
            for copy in down_copies(step):
                copy.wait_recv()

    for d in range(2, n):
        @pl.when(me == d)
        def _():
            for piece in range(SPLIT):
                for copy in up_copies(d, piece, True):
                    copy.wait_recv()

    for step in range(1, n):
        @pl.when(me >= step)
        def _():
            oq_copy(step).wait_send()

        @pl.when((me >= step) & (me < n - 1))
        def _():
            oq_up(step).wait_send()

    @pl.when((me == 0) | relay_up)
    def _():
        oq_first(0, up, True).wait_send()

    @pl.when(relay_down)
    def _():
        oq_first(1, below, True).wait_send()

    @pl.when(me == 0)
    def _():
        def drain(c, carry):
            for copy in anchor_copies(c, True):
                copy.wait_send()
            return carry

        lax.fori_loop(0, chunks, drain, 0)

    @pl.when((me > 0) & (me < n - 1))
    def _():
        def drain(c, carry):
            for copy in anchor_copies(c, False):
                copy.wait_send()
            return carry

        lax.fori_loop(0, chunks, drain, 0)

    for step in range(1, n):
        @pl.when(me >= step)
        def _():
            for copy in down_copies(step):
                copy.wait_send()

    for d in range(2, n):
        @pl.when((me > 0) & (me < d))
        def _():
            for piece in range(SPLIT):
                for copy in up_copies(d, piece, False):
                    copy.wait_send()


def merge(
    n,
    ctx_ref, rx_p, rx_s, mine_ref, q_ref, ak_ref, avt_ref, acc_ref, m_ref,
    ctx_hbm, opt_ref,
    tail_ref, sem, tail_sem,
):
    me = lax.axis_index("blk")
    rows, width = ctx_ref.shape
    heads = width // HD
    tile = rows // 2
    base = heads - TAIL
    g = heads // GROUP - 1
    span_rows = rows // HALVES
    keys = pl.ds((HALVES - 1) * span_rows, span_rows)
    part = rows // WRITES

    def early_copies():
        return [
            pltpu.make_async_copy(
                ctx_ref.at[pl.ds(i * part, part), pl.ds(0, base * HD)],
                ctx_hbm.at[pl.ds(i * part, part), pl.ds(0, base * HD)],
                sem.at[i],
            )
            for i in range(WRITES)
        ]

    def tail_copy(i, src):
        cols = pl.ds(i * PAIR * HD, PAIR * HD)
        return pltpu.make_async_copy(
            src.at[:, cols if src is tail_ref else pl.ds((base + i * PAIR) * HD, PAIR * HD)],
            ctx_hbm.at[:, pl.ds((base + i * PAIR) * HD, PAIR * HD)],
            tail_sem.at[i],
        )

    if base:
        for copy in early_copies():
            copy.start()

    top = rx_s[0]
    for b in range(1, n):
        top = jnp.maximum(top, rx_s[b])
    weights = [jnp.exp(rx_s[b] - top) for b in range(n)]
    scale = 1.0 / functools.reduce(jnp.add, weights)
    weights = [x * scale for x in weights]
    occupied = mine_ref[...] > 0.0

    def merge_head(h):
        cols = pl.ds(h * HD, HD)
        merged = jnp.zeros((CAP, HD), jnp.float32)
        for b in range(n):
            merged = merged + weights[b][:, h : h + 1] * rx_p[b, :, cols].astype(jnp.float32)
        opt_ref[:, cols] = jnp.where(occupied, merged, 0.0).astype(jnp.bfloat16)

    @pl.when(me == 0)
    def _():
        for i in range(TAIL // PAIR):
            tail_copy(i, ctx_ref).start()
        for h in range(heads):
            merge_head(h)

    @pl.when(me > 0)
    def _():
        units = [(j, t) for j in range(TAIL) for t in range(2)]
        raw, tops, probs = {}, {}, {}

        def scores(u):
            j, t = units[u]
            span = pl.ds(t * tile, tile)
            query = q_ref[span, pl.ds((base + j) * HD, HD)]
            raw[u] = dot_nt(ak_ref[keys, pl.ds(2 * g * HD, HD)], query)
            high = jnp.max(raw[u], axis=0, keepdims=True) * COEF
            tops[u] = jnp.maximum(high, m_ref[base + j, pl.ds(0, 1), span])

        def soften(u):
            probs[u] = jnp.exp2(raw.pop(u) * COEF - tops[u]).astype(jnp.bfloat16)

        def gather(u):
            j, t = units[u]
            span = pl.ds(t * tile, tile)
            alpha = jnp.exp2(m_ref[base + j, pl.ds(0, 1), span] - tops[u])
            acc = dot_nn(avt_ref[g, :, keys], probs.pop(u)) + alpha * acc_ref[base + j, :, span]
            out = (acc[:HD] * (1.0 / acc[HD : HD + 1])).T.astype(jnp.bfloat16)
            tail_ref[span, pl.ds(j * HD, HD)] = out
            for h in range(u * heads // len(units), (u + 1) * heads // len(units)):
                merge_head(h)
            if t == 1 and j % PAIR == PAIR - 1:
                tail_copy(j // PAIR, tail_ref).start()

        staged(len(units), scores, soften, gather)

    if base:
        for copy in early_copies():
            copy.wait()
    for i in range(TAIL // PAIR):
        tail_copy(i, ctx_ref).wait()


def body(ctx_query, ctx_key, ctx_value, opt_query, opt_owner, opt_slot, opt_length):
    n = lax.axis_size("blk")
    rows, width = ctx_query.shape
    heads = width // HD
    kvs = ctx_key.shape[1] // HD
    opts = opt_length.shape[0]
    chunks = HALVES * PIECES * kvs
    bf16, f32 = jnp.bfloat16, jnp.float32
    dma = pltpu.SemaphoreType.DMA
    hbm = pl.BlockSpec(memory_space=pltpu.HBM)
    vmem = pl.BlockSpec(memory_space=pltpu.VMEM)
    length, owner, slot = (x.reshape(1, opts) for x in (opt_length, opt_owner, opt_slot))
    kept = 2 * width * (2 * rows + n * CAP) + 4 * HD * CAP * (n + 1)
    kept += 2 * rows * kvs * (2 * HD + VR) + 4 * (heads + 1) * (VR + 8) * rows
    state = pl.pallas_call(
        functools.partial(attend, n),
        out_shape=(
            pltpu.VMEM((rows, width), bf16),
            pltpu.VMEM((n, CAP, width), bf16),
            pltpu.VMEM((n, CAP, HD), f32),
            pltpu.VMEM((CAP, HD), f32),
            pltpu.VMEM((rows, width), bf16),
            pltpu.VMEM((rows, 2 * kvs * HD), bf16),
            pltpu.VMEM((kvs, VR, rows), bf16),
            pltpu.VMEM((heads + 1, VR, rows), f32),
            pltpu.VMEM((heads + 1, 8, rows), f32),
        ),
        in_specs=[hbm] * 7,
        out_specs=(vmem,) * 9,
        scratch_shapes=[
            pltpu.VMEM((rows, kvs * HD), bf16),
            pltpu.VMEM((rows, kvs * HD), bf16),
            pltpu.VMEM((kvs, VR, rows), bf16),
            pltpu.VMEM((opts, width), bf16),
            pltpu.VMEM((rows // HALVES, rows), f32),
            pltpu.VMEM((rows // HALVES, rows), f32),
            pltpu.VMEM((rows // HALVES, rows), bf16),
            pltpu.VMEM((rows // HALVES, rows), bf16),
            pltpu.VMEM((16, rows), f32),
            pltpu.VMEM((16, rows), f32),
            pltpu.VMEM((opts, width), bf16),
            pltpu.VMEM((opts, HD), f32),
            pltpu.VMEM((n * CAP, width), bf16),
            pltpu.VMEM((n * CAP, HD), f32),
            pltpu.VMEM((n, CAP, width), bf16),
            pltpu.VMEM((n, CAP, HD), f32),
            pltpu.VMEM((24, opts), jnp.int32),
            dma((3,)), dma((heads // PAIR,)), dma(()), dma(()), dma(()),
            dma((n - 1,)), dma((n - 1,)), dma((n - 1,)), dma((n - 1,)), dma((2,)), dma(()),
            dma((chunks,)), dma((chunks,)), dma((chunks,)),
            dma((n - 1,)), dma((n - 1,)), dma((n - 1,)), dma((n - 1,)),
            dma((n, SPLIT)), dma((n, SPLIT)), dma((n,)), dma((n,)),
            pltpu.SemaphoreType.REGULAR, pltpu.SemaphoreType.REGULAR,
        ],
        compiler_params=pltpu.CompilerParams(
            collective_id=0, has_side_effects=True, vmem_limit_bytes=LIMIT - kept
        ),
        name="star",
    )(ctx_query, ctx_key, ctx_value, opt_query, length, owner, slot)
    return pl.pallas_call(
        functools.partial(merge, n),
        out_shape=(
            jax.ShapeDtypeStruct((rows, width), bf16),
            jax.ShapeDtypeStruct((CAP, width), bf16),
        ),
        in_specs=[vmem] * 9,
        out_specs=(hbm, vmem),
        scratch_shapes=[
            pltpu.VMEM((rows, TAIL * HD), bf16),
            dma((WRITES,)),
            dma((TAIL // PAIR,)),
        ],
        compiler_params=pltpu.CompilerParams(vmem_limit_bytes=16 * 1024 * 1024),
        name="merge",
    )(*state)


def solution(mesh):
    return jax.shard_map(
        body,
        mesh=mesh,
        in_specs=(
            P(("groups", "blk"), "head"),
            P(("groups", "blk"), "head"),
            P(("groups", "blk"), "head"),
            P(("groups", "blk"), "head"),
            P("groups"),
            P("groups"),
            P("groups"),
        ),
        out_specs=(P(("groups", "blk"), "head"), P(("groups", "blk"), "head")),
        check_vma=False,
    )
```

```python
import functools
import math

import jax
import jax.numpy as jnp
from jax import lax
from jax.experimental import pallas as pl
from jax.experimental.pallas import tpu as pltpu
from jax.sharding import PartitionSpec as P

HD = 128
HQ = 64
KVH = 8
CAP = 32
GROUP = HQ // KVH
MESH = pl.DeviceIdType.MESH
NEG = -1e30
LN2 = math.log(2.0)
COEF = HD**-0.5 / LN2
PAIR = 2
HALVES = 2
PIECES = 4
VR = HD + 16
PER = GROUP // 2
WRITES = 8
LEAD = 2
SPLIT = 2
TAIL = 6
LIMIT = 65100 * 1024
GREET = 0


def dot_nt(a, b):
    return lax.dot_general(a, b, (((1,), (1,)), ((), ())), preferred_element_type=jnp.float32)


def dot_nn(a, b, precision=None):
    return lax.dot_general(
        a, b, (((1,), (0,)), ((), ())), preferred_element_type=jnp.float32, precision=precision
    )


def staged(count, scores, soften, gather):
    for k in range(count + 2):
        if k < count:
            scores(k)
        if 0 <= k - 1 < count:
            soften(k - 1)
        if 0 <= k - 2 < count:
            gather(k - 2)


def attend(
    n,
    q_hbm, k_hbm, v_hbm, oq_hbm, len_hbm, owner_hbm, slot_hbm,
    ctx_ref, rx_p, rx_s, mine_ref, q_ref, ak_ref, avt_ref, acc_ref, m_ref,
    k_ref, v_ref, vt_ref, oq_ref,
    raw_a, raw_b, prob_a, prob_b, top_a, top_b, part_ref, stat_ref, pbuf, sbuf, up_p, up_s, place_ref,
    place_sem, q_sem, k_sem, v_sem, o_sem,
    oq_send, oq_recv, ou_send, ou_recv, oz_send, oz_recv, ak_send, ak_recv, av_send,
    p_send, p_recv, s_send, s_recv, pu_send, pu_recv, su_send, su_recv, low_sem, near_sem,
):
    me = lax.axis_index("blk")
    rows = q_ref.shape[0]
    heads = q_ref.shape[1] // HD
    kvs = k_ref.shape[1] // HD
    entry = oq_hbm.shape[0]
    opts = oq_ref.shape[0]
    pairs = heads // PAIR
    tile = rows // 2
    span_rows = rows // HALVES
    chunk = span_rows // PIECES
    chunks = kvs * HALVES * PIECES

    def q_copy(i):
        cols = pl.ds(pl.multiple_of(i * PAIR * HD, PAIR * HD), PAIR * HD)
        return pltpu.make_async_copy(q_hbm.at[:, cols], q_ref.at[:, cols], q_sem.at[i])

    k_copy = pltpu.make_async_copy(k_hbm, k_ref, k_sem)
    v_copy = pltpu.make_async_copy(v_hbm, v_ref, v_sem)
    own = pl.ds(pl.multiple_of(me * entry, entry), entry)
    o_copy = pltpu.make_async_copy(oq_hbm, oq_ref.at[own], o_sem)

    place_copies = [
        pltpu.make_async_copy(src, place_ref.at[pl.ds(8 * i, 1)], place_sem.at[i])
        for i, src in enumerate((len_hbm, owner_hbm, slot_hbm))
    ]
    barrier = pltpu.get_barrier_semaphore()
    up = lax.rem(me + 1, n)
    below = lax.rem(me - 1 + n, n)

    @pl.when(me < n - 1)
    def _():
        pl.semaphore_signal(barrier, inc=1, device_id={"blk": up}, device_id_type=MESH)

    @pl.when(me > 0)
    def _():
        pl.semaphore_signal(barrier, inc=1, device_id={"blk": below}, device_id_type=MESH)

    k_copy.start()
    q_copy(0).start()
    v_copy.start()
    for i in range(1, pairs):
        q_copy(i).start()
    o_copy.start()
    for copy in place_copies:
        copy.start()

    def oq_copy(step):
        return pltpu.make_async_remote_copy(
            src_ref=oq_hbm,
            dst_ref=oq_ref.at[own],
            send_sem=oq_send.at[step - 1],
            recv_sem=oq_recv.at[step - 1],
            device_id={"blk": lax.rem(me - step + n, n)},
            device_id_type=MESH,
        )

    def oq_up(step):
        at = lax.rem(me + 1 - step + n, n)
        span = pl.ds(pl.multiple_of(at * entry, entry), entry)
        return pltpu.make_async_remote_copy(
            src_ref=oq_hbm if step == 1 else oq_ref.at[span],
            dst_ref=oq_ref.at[span],
            send_sem=ou_send.at[step - 1],
            recv_sem=ou_recv.at[step - 1],
            device_id={"blk": up},
            device_id_type=MESH,
        )

    def oq_pass(step):
        @pl.when(me > step)
        def _():
            oq_up(step).wait_recv()

        @pl.when((me > step) & (me < n - 1))
        def _():
            oq_up(step + 1).start()

    first_rows = pl.ds(0, entry)

    hub = min(2, n - 1)

    def oq_first(index, to, relay):
        return pltpu.make_async_remote_copy(
            src_ref=oq_ref.at[first_rows] if relay else oq_hbm,
            dst_ref=oq_ref.at[first_rows],
            send_sem=oz_send.at[index],
            recv_sem=oz_recv,
            device_id={"blk": to},
            device_id_type=MESH,
        )

    def head_cols(h):
        return pl.ds(pl.multiple_of(h * HD, HD), HD)

    def anchor_copies(c, first):
        g = c // (HALVES * PIECES)
        r = lax.rem(c, HALVES * PIECES)
        span = pl.ds(pl.multiple_of(r * chunk, chunk), chunk)

        def copy(src, cols, send):
            return pltpu.make_async_remote_copy(
                src_ref=src,
                dst_ref=ak_ref.at[span, cols],
                send_sem=send.at[c],
                recv_sem=ak_recv.at[c],
                device_id={"blk": up},
                device_id_type=MESH,
            )

        if not first:
            both = pl.ds(pl.multiple_of(2 * g * HD, 2 * HD), 2 * HD)
            return (copy(ak_ref.at[span, both], both, ak_send),)
        return (
            copy(k_hbm.at[span, head_cols(g)], head_cols(2 * g), ak_send),
            copy(v_hbm.at[span, head_cols(g)], head_cols(2 * g + 1), av_send),
        )

    def send_anchor(low, high):
        def send(c, carry):
            for copy in anchor_copies(c, True):
                copy.start()
            return carry

        lax.fori_loop(low, high, send, 0)

    def greet():
        @pl.when((me > 0) & (me < n - 1))
        def _():
            pl.semaphore_wait(barrier, 2)

        @pl.when((me == 0) | (me == n - 1))
        def _():
            pl.semaphore_wait(barrier, 1)

        @pl.when(me == 0)
        def _():
            send_anchor(0, LEAD)

        @pl.when(me > 1)
        def _():
            pl.semaphore_wait(low_sem, 1)

        @pl.when((me > 0) & (me < n - 1))
        def _():
            pl.semaphore_signal(low_sem, inc=1, device_id={"blk": up}, device_id_type=MESH)

        @pl.when((me == 1) & (me < n - 1))
        def _():
            pl.semaphore_signal(near_sem, inc=1, device_id={"blk": below}, device_id_type=MESH)

        if n > 2:
            @pl.when(me == 0)
            def _():
                pl.semaphore_wait(near_sem, 1)

        @pl.when(me == 0)
        def _():
            oq_first(0, hub, False).start()
            send_anchor(LEAD, chunks)

        @pl.when((me > 0) & (me < n - 1))
        def _():
            oq_up(1).start()

        for step in range(1, n):
            @pl.when(me >= step)
            def _():
                oq_copy(step).start()

    def forward(c):
        for copy in anchor_copies(c, False):
            copy.wait_recv()

        @pl.when(me < n - 1)
        def _():
            for copy in anchor_copies(c, False):
                copy.start()

    ones = jnp.ones((VR - HD, rows), jnp.bfloat16)
    k_copy.wait()
    v_copy.wait()
    for g in range(kvs):
        vt_ref[g, :HD, :] = v_ref[:, g * HD : (g + 1) * HD].T
        vt_ref[g, HD:, :] = ones
        avt_ref[g, HD:, :] = ones

    causal = lax.broadcasted_iota(jnp.int32, (tile, tile), 0) <= lax.broadcasted_iota(
        jnp.int32, (tile, tile), 1
    )

    def local_heads(hs):
        units = [(h, t) for h in hs for t in range(2)]
        raw, tops, probs = {}, {}, {}

        def scores(u):
            h, t = units[u]
            query = q_ref[pl.ds(t * tile, tile), head_cols(h)]
            score = dot_nt(k_ref[pl.ds(0, (t + 1) * tile), head_cols(h // GROUP)], query)
            parts = [score[j * tile : (j + 1) * tile] for j in range(t + 1)]
            parts[t] = jnp.where(causal, parts[t], NEG)
            top = functools.reduce(jnp.maximum, [jnp.max(x, axis=0, keepdims=True) for x in parts])
            tops[u] = top * COEF
            raw[u] = parts

        def soften(u):
            probs[u] = [jnp.exp2(x * COEF - tops[u]).astype(jnp.bfloat16) for x in raw.pop(u)]

        def gather(u):
            h, t = units[u]
            span = pl.ds(t * tile, tile)
            prob = jnp.concatenate(probs.pop(u), axis=0)
            acc_ref[h, :, span] = dot_nn(vt_ref[h // GROUP, :, pl.ds(0, (t + 1) * tile)], prob)
            m_ref[h, :, span] = jnp.broadcast_to(tops[u], (8, tile))

        staged(len(units), scores, soften, gather)

    def finish(h, span, acc):
        ctx_ref[span, head_cols(h)] = (acc[:HD] * (1.0 / acc[HD : HD + 1])).T.astype(jnp.bfloat16)

    units = heads * HALVES - TAIL
    per = PER

    def unit_place(u):
        block = u // GROUP
        g = block // HALVES
        half = lax.rem(block, HALVES)
        keys = pl.ds(pl.multiple_of(half * span_rows, span_rows), span_rows)
        return g, g * GROUP + lax.rem(u, GROUP), keys

    def unit_scores(u, raw, top):
        g, h, keys = unit_place(jnp.minimum(u, units - 1))
        for t in range(2):
            span = pl.ds(t * tile, tile)
            score = dot_nt(ak_ref[keys, head_cols(2 * g)], q_ref[span, head_cols(h)])
            raw[:, span] = score
            high = jnp.max(score, axis=0, keepdims=True) * COEF
            high = jnp.maximum(high, m_ref[h, pl.ds(0, 1), span])
            top[pl.ds(0, 8), span] = jnp.broadcast_to(high, (8, tile))

    def unit_soften(raw, top, prob):
        for t in range(2):
            span = pl.ds(t * tile, tile)
            high = top[pl.ds(0, 1), span]
            prob[:, span] = jnp.exp2(raw[:, span] * COEF - high).astype(jnp.bfloat16)
        top[pl.ds(8, 8), :] = top[pl.ds(0, 8), :]

    def unit_gather(u, prob, top, last):
        g, h, keys = unit_place(jnp.maximum(u, 0))
        slot = jnp.where(u < 0, heads, h)
        for t in range(2):
            span = pl.ds(t * tile, tile)
            high = top[pl.ds(8, 1), span]
            alpha = jnp.exp2(m_ref[slot, pl.ds(0, 1), span] - high)
            acc = dot_nn(avt_ref[g, :, keys], prob[:, span]) + alpha * acc_ref[slot, :, span]
            if last:
                finish(h, span, acc)
            else:
                acc_ref[slot, :, span] = acc
                m_ref[slot, :, span] = jnp.broadcast_to(high, (8, tile))

    def trip(i, last):
        unit_gather(2 * i - 2, prob_a, top_a, last)
        unit_soften(raw_b, top_b, prob_b)
        unit_scores(2 * i, raw_a, top_a)
        unit_gather(2 * i - 1, prob_b, top_b, last)
        unit_soften(raw_a, top_a, prob_a)
        unit_scores(2 * i + 1, raw_b, top_b)

    for copy in place_copies:
        copy.wait()
    length = place_ref[pl.ds(0, 1), :].astype(jnp.float32)
    dest = place_ref[pl.ds(8, 1), :] * CAP + place_ref[pl.ds(16, 1), :]

    def opt_attend(queries, counts, key, value_t):
        size = queries.shape[0]
        stacked = jnp.concatenate([queries[:, j * HD : (j + 1) * HD] for j in range(GROUP)], axis=0)
        score = dot_nt(key, stacked)
        if counts is not None:
            spot = lax.broadcasted_iota(jnp.int32, score.shape, 0).astype(jnp.float32)
            score = jnp.where(spot < counts, score, NEG)
        top = jnp.max(score, axis=0, keepdims=True) * COEF
        acc = dot_nn(value_t, jnp.exp2(score * COEF - top).astype(jnp.bfloat16))
        total = acc[HD : HD + 1]
        part = acc[:HD] * (1.0 / total)
        stat = top * LN2 + jnp.log(total)
        if counts is not None:
            live = counts > 0.0
            part = jnp.where(live, part, 0.0)
            stat = jnp.where(live, stat, NEG)
        part = part.T.astype(jnp.bfloat16)
        stat = jnp.broadcast_to(stat, (HD, stat.shape[1])).T
        return (
            [part[j * size : (j + 1) * size] for j in range(GROUP)],
            [stat[j * size : (j + 1) * size] for j in range(GROUP)],
        )

    step_rows = min(opts, 64)
    lane_opts = GROUP * step_rows

    def options_group(g):
        lanes = lax.broadcasted_iota(jnp.int32, (step_rows, HD), 1)
        for base in range(0, opts, step_rows):
            span = pl.ds(base, step_rows)
            pick = lax.broadcasted_iota(jnp.int32, (opts, lane_opts), 0) - base
            pick = pick == lax.rem(lax.broadcasted_iota(jnp.int32, (opts, lane_opts), 1), step_rows)
            spread = dot_nn(
                jnp.broadcast_to(length, (8, opts)), pick.astype(jnp.float32), lax.Precision.HIGHEST
            )
            counts = jnp.clip(spread[:1] - (me * rows).astype(jnp.float32), 0.0, float(rows))
            queries = oq_ref[span, pl.ds(g * GROUP * HD, GROUP * HD)]
            parts, tops = opt_attend(queries, counts, k_ref[:, pl.ds(g * HD, HD)], vt_ref[g])
            stats = jnp.zeros((step_rows, HD), jnp.float32) if g == 0 else stat_ref[span, :]
            for j in range(GROUP):
                h = g * GROUP + j
                part_ref[span, pl.ds(h * HD, HD)] = parts[j]
                stats = jnp.where(lanes == h, tops[j], stats)
            stat_ref[span, :] = stats

    slots = lax.broadcasted_iota(jnp.int32, (CAP, opts), 0)
    mine = (slots + me * CAP == dest).astype(jnp.float32)
    mine_ref[...] = jnp.broadcast_to(jnp.sum(mine, axis=1, keepdims=True), (CAP, HD))

    def options_scatter():
        for d in range(n):
            hot = (slots + d * CAP == dest).astype(jnp.float32)
            span = pl.ds(d * CAP, CAP)
            pbuf[span, :] = dot_nn(hot.astype(jnp.bfloat16), part_ref[...]).astype(jnp.bfloat16)
            sbuf[span, :] = dot_nn(hot, stat_ref[...], lax.Precision.HIGHEST)

    def down_copies(step):
        to = lax.rem(me - step + n, n)
        span = pl.ds(pl.multiple_of(to * CAP, CAP), CAP)
        return (
            pltpu.make_async_remote_copy(
                src_ref=pbuf.at[span],
                dst_ref=rx_p.at[me],
                send_sem=p_send.at[step - 1],
                recv_sem=p_recv.at[step - 1],
                device_id={"blk": to},
                device_id_type=MESH,
            ),
            pltpu.make_async_remote_copy(
                src_ref=sbuf.at[span],
                dst_ref=rx_s.at[me],
                send_sem=s_send.at[step - 1],
                recv_sem=s_recv.at[step - 1],
                device_id={"blk": to},
                device_id_type=MESH,
            ),
        )

    share = heads // SPLIT

    def up_copies(d, piece, final):
        span = pl.ds(d * CAP, CAP)
        cols = pl.ds(piece * share * HD, share * HD)
        copies = [
            pltpu.make_async_remote_copy(
                src_ref=pbuf.at[span, cols],
                dst_ref=rx_p.at[me, :, cols] if final else up_p.at[d, :, cols],
                send_sem=pu_send.at[d, piece],
                recv_sem=pu_recv.at[d, piece],
                device_id={"blk": up},
                device_id_type=MESH,
            )
        ]
        if piece == 0:
            copies.append(
                pltpu.make_async_remote_copy(
                    src_ref=sbuf.at[span],
                    dst_ref=rx_s.at[me] if final else up_s.at[d],
                    send_sem=su_send.at[d],
                    recv_sem=su_recv.at[d],
                    device_id={"blk": up},
                    device_id_type=MESH,
                )
            )
        return copies

    def send_down():
        for step in range(n - 1, 0, -1):
            @pl.when(me >= step)
            def _():
                for copy in down_copies(step):
                    copy.start()

    def combine(d):
        span = pl.ds(d * CAP, CAP)
        final = me == d - 1
        for piece in range(SPLIT):
            for copy in up_copies(d, piece, False):
                copy.wait_recv()
            if piece == 0:
                low, own_stat = up_s[d], sbuf[span, :]
                top = jnp.maximum(low, own_stat)
                low, own_stat = jnp.exp(low - top), jnp.exp(own_stat - top)
                total = low + own_stat
                sbuf[span, :] = top + jnp.log(total)
                low, own_stat = low / total, own_stat / total
            for h in range(piece * share, (piece + 1) * share):
                cols = pl.ds(h * HD, HD)
                mixed = low[:, h : h + 1] * up_p[d, :, cols].astype(jnp.float32)
                mixed = mixed + own_stat[:, h : h + 1] * pbuf[span, cols].astype(jnp.float32)
                pbuf[span, cols] = mixed.astype(jnp.bfloat16)

            @pl.when(final)
            def _():
                for copy in up_copies(d, piece, True):
                    copy.start()

            @pl.when(jnp.logical_not(final))
            def _():
                for copy in up_copies(d, piece, False):
                    copy.start()

    def send_up_first():
        for d in range(n - 1, 2, -1):
            for piece in range(SPLIT):
                for copy in up_copies(d, piece, False):
                    copy.start()

    def send_up_rest():
        for d in range(n - 1, 2, -1):
            @pl.when(me < d)
            def _():
                combine(d)

    def send_up_last():
        for piece in range(SPLIT):
            for copy in up_copies(hub, piece, True):
                copy.start()

    def options_anchor(g, key_of, value_of, stride):
        hot = mine.astype(jnp.bfloat16)
        lanes = lax.broadcasted_iota(jnp.int32, (CAP, HD), 1)
        queries = dot_nn(hot, oq_ref[:, pl.ds(pl.multiple_of(g * GROUP * HD, GROUP * HD), GROUP * HD)]).astype(jnp.bfloat16)
        parts, tops = opt_attend(queries, None, key_of[:, head_cols(stride * g)], value_of[g])
        stats = rx_s[0]
        for j in range(GROUP):
            h = g * GROUP + j
            rx_p[0, :, head_cols(h)] = parts[j]
            stats = jnp.where(lanes == h, tops[j], stats)
        rx_s[0] = stats

    @pl.when(me == 0)
    def _():
        greet()

    def local_pair(i, carry):
        q_copy(i).wait()
        local_heads([i * PAIR + j for j in range(PAIR)])

        @pl.when((i == GREET) & (me > 0))
        def _():
            greet()

        @pl.when(i == max(pairs - 3, 0))
        def _():
            oq_pass(1)

        @pl.when((i >= pairs - 2) & (me == 1) & (me < n - 1))
        def _():
            forward(i - (pairs - 2))

        return carry

    lax.fori_loop(0, pairs, local_pair, 0)

    relay_down = (me == hub) & (me > 1)
    relay_up = (me >= hub) & (me < n - 1)

    def oq_wait():
        o_copy.wait()

        @pl.when(me > 0)
        def _():
            oq_first(0, up, True).wait_recv()

        @pl.when(relay_up)
        def _():
            oq_first(0, up, True).start()

        @pl.when(relay_down)
        def _():
            oq_first(1, below, True).start()

        for step in range(2, n - 1):
            oq_pass(step)
        for step in range(1, n):
            @pl.when(me + step < n)
            def _():
                oq_copy(step).wait_recv()

    @pl.when(me == 0)
    def _():
        oq_wait()

        def whole(h, carry):
            for t in range(2):
                span = pl.ds(t * tile, tile)
                finish(h, span, acc_ref[h, :, span])
            return carry

        lax.fori_loop(0, heads, whole, 0)
        rx_s[0] = jnp.zeros_like(rx_s[0])
        for g in range(kvs):
            options_anchor(g, k_ref, vt_ref, 1)

    @pl.when(me > 0)
    def _():

        def forward_range(low, high):
            def one(c, carry):
                forward(c)
                return carry

            lax.fori_loop(low, high, one, 0)

        @pl.when(me == 1)
        def _():
            forward_range(jnp.where(me < n - 1, 2, 0), PIECES)

        steps = units // 2 + 1
        early = min(PER + 1, steps - 1)
        sent = min(early + PIECES, steps - 1)
        closing = min(chunks - PIECES, steps - 1)

        def forward_early(c):
            @pl.when((me == 1) & (c < chunks))
            def _():
                forward(c)

        def options_all():
            oq_wait()
            for g in range(kvs):
                options_group(g)
                forward_early(PIECES + early + g)
            options_scatter()
            forward_early(PIECES + early + kvs)
            send_down()
            own_slots = pl.ds(pl.multiple_of(me * CAP, CAP), CAP)
            rx_p[me] = pbuf[own_slots, :]
            rx_s[me] = sbuf[own_slots, :]
            for b in range(1, n - 2):
                @pl.when(b < me - 1)
                def _():
                    rx_p[b] = jnp.zeros_like(rx_p[b])
                    rx_s[b] = jnp.full_like(rx_s[b], NEG)


            @pl.when(me > 1)
            def _():
                forward_range(0, PIECES)

        turn = jnp.where(me == 1, early, 0)
        rx_s[0] = jnp.zeros_like(rx_s[0])

        def turn_values(u):
            g, _, keys = unit_place(u)
            avt_ref[g, :HD, keys] = ak_ref[keys, head_cols(2 * g + 1)].T

        def anchor_step(i, carry):
            @pl.when(i == turn)
            def _():
                options_all()

            @pl.when((lax.rem(i, per) == 0) & (2 * i < units))
            def _():
                turn_values(2 * i)

            last = lax.rem((jnp.maximum(i, 1) - 1) // per, HALVES) == HALVES - 1

            @pl.when(last)
            def _():
                trip(i, True)

            @pl.when(jnp.logical_not(last))
            def _():
                trip(i, False)

            following = PIECES + i + jnp.where((me == 1) & (i >= early), kvs + 1, 0)

            @pl.when(following < chunks)
            def _():
                forward(following)

            @pl.when((me == 1) & (i == sent))
            def _():
                send_up_first()

            @pl.when((me == 1) & (me < n - 1) & (i == max(closing, sent)))
            def _():
                send_up_last()

            @pl.when((me > 1) & (me < n - 1) & (i == closing))
            def _():
                send_up_rest()

            @pl.when((lax.rem(i, per * HALVES) == per + 1) & (me == n - 1))
            def _():
                options_anchor(i // (per * HALVES), ak_ref, avt_ref, 2)

            return carry

        lax.fori_loop(0, steps, anchor_step, 0)

        def options_rest(g, carry):
            options_anchor(g, ak_ref, avt_ref, 2)
            return carry

        @pl.when(me < n - 1)
        def _():
            lax.fori_loop(0, kvs, options_rest, 0)

    for step in range(1, n):
        @pl.when(me + step < n)
        def _():
            for copy in down_copies(step):
                copy.wait_recv()

    for d in range(2, n):
        @pl.when(me == d)
        def _():
            for piece in range(SPLIT):
                for copy in up_copies(d, piece, True):
                    copy.wait_recv()

    for step in range(1, n):
        @pl.when(me >= step)
        def _():
            oq_copy(step).wait_send()

        @pl.when((me >= step) & (me < n - 1))
        def _():
            oq_up(step).wait_send()

    @pl.when((me == 0) | relay_up)
    def _():
        oq_first(0, up, True).wait_send()

    @pl.when(relay_down)
    def _():
        oq_first(1, below, True).wait_send()

    @pl.when(me == 0)
    def _():
        def drain(c, carry):
            for copy in anchor_copies(c, True):
                copy.wait_send()
            return carry

        lax.fori_loop(0, chunks, drain, 0)

    @pl.when((me > 0) & (me < n - 1))
    def _():
        def drain(c, carry):
            for copy in anchor_copies(c, False):
                copy.wait_send()
            return carry

        lax.fori_loop(0, chunks, drain, 0)

    for step in range(1, n):
        @pl.when(me >= step)
        def _():
            for copy in down_copies(step):
                copy.wait_send()

    for d in range(2, n):
        @pl.when((me > 0) & (me < d))
        def _():
            for piece in range(SPLIT):
                for copy in up_copies(d, piece, False):
                    copy.wait_send()


def merge(
    n,
    ctx_ref, rx_p, rx_s, mine_ref, q_ref, ak_ref, avt_ref, acc_ref, m_ref,
    ctx_hbm, opt_hbm,
    tail_ref, opt_ref, sem, tail_sem, opt_sem,
):
    me = lax.axis_index("blk")
    rows, width = ctx_ref.shape
    heads = width // HD
    tile = rows // 2
    base = heads - TAIL
    g = heads // GROUP - 1
    span_rows = rows // HALVES
    keys = pl.ds((HALVES - 1) * span_rows, span_rows)
    part = rows // WRITES

    def early_copies():
        return [
            pltpu.make_async_copy(
                ctx_ref.at[pl.ds(i * part, part), pl.ds(0, base * HD)],
                ctx_hbm.at[pl.ds(i * part, part), pl.ds(0, base * HD)],
                sem.at[i],
            )
            for i in range(WRITES)
        ]

    def tail_copy(i, src):
        cols = pl.ds(i * PAIR * HD, PAIR * HD)
        return pltpu.make_async_copy(
            src.at[:, cols if src is tail_ref else pl.ds((base + i * PAIR) * HD, PAIR * HD)],
            ctx_hbm.at[:, pl.ds((base + i * PAIR) * HD, PAIR * HD)],
            tail_sem.at[i],
        )

    if base:
        for copy in early_copies():
            copy.start()

    top = rx_s[0]
    for b in range(1, n):
        top = jnp.maximum(top, rx_s[b])
    weights = [jnp.exp(rx_s[b] - top) for b in range(n)]
    scale = 1.0 / functools.reduce(jnp.add, weights)
    weights = [x * scale for x in weights]
    occupied = mine_ref[...] > 0.0

    opt_copy = pltpu.make_async_copy(opt_ref, opt_hbm, opt_sem)

    def merge_head(h):
        cols = pl.ds(h * HD, HD)
        merged = jnp.zeros((CAP, HD), jnp.float32)
        for b in range(n):
            merged = merged + weights[b][:, h : h + 1] * rx_p[b, :, cols].astype(jnp.float32)
        opt_ref[:, cols] = jnp.where(occupied, merged, 0.0).astype(jnp.bfloat16)

    @pl.when(me == 0)
    def _():
        for i in range(TAIL // PAIR):
            tail_copy(i, ctx_ref).start()
        for h in range(heads):
            merge_head(h)
        opt_copy.start()

    @pl.when(me > 0)
    def _():
        units = [(j, t) for j in range(TAIL) for t in range(2)]
        raw, tops, probs = {}, {}, {}

        def scores(u):
            j, t = units[u]
            span = pl.ds(t * tile, tile)
            query = q_ref[span, pl.ds((base + j) * HD, HD)]
            raw[u] = dot_nt(ak_ref[keys, pl.ds(2 * g * HD, HD)], query)
            high = jnp.max(raw[u], axis=0, keepdims=True) * COEF
            tops[u] = jnp.maximum(high, m_ref[base + j, pl.ds(0, 1), span])

        def soften(u):
            probs[u] = jnp.exp2(raw.pop(u) * COEF - tops[u]).astype(jnp.bfloat16)

        def gather(u):
            j, t = units[u]
            span = pl.ds(t * tile, tile)
            alpha = jnp.exp2(m_ref[base + j, pl.ds(0, 1), span] - tops[u])
            acc = dot_nn(avt_ref[g, :, keys], probs.pop(u)) + alpha * acc_ref[base + j, :, span]
            out = (acc[:HD] * (1.0 / acc[HD : HD + 1])).T.astype(jnp.bfloat16)
            tail_ref[span, pl.ds(j * HD, HD)] = out
            half = len(units) // 2
            for h in range(min(u, half) * heads // half, min(u + 1, half) * heads // half):
                merge_head(h)
            if u == half - 1:
                opt_copy.start()
            if t == 1 and j % PAIR == PAIR - 1:
                tail_copy(j // PAIR, tail_ref).start()

        staged(len(units), scores, soften, gather)

    if base:
        for copy in early_copies():
            copy.wait()
    for i in range(TAIL // PAIR):
        tail_copy(i, ctx_ref).wait()
    opt_copy.wait()


def body(ctx_query, ctx_key, ctx_value, opt_query, opt_owner, opt_slot, opt_length):
    n = lax.axis_size("blk")
    rows, width = ctx_query.shape
    heads = width // HD
    kvs = ctx_key.shape[1] // HD
    opts = opt_length.shape[0]
    chunks = HALVES * PIECES * kvs
    bf16, f32 = jnp.bfloat16, jnp.float32
    dma = pltpu.SemaphoreType.DMA
    hbm = pl.BlockSpec(memory_space=pltpu.HBM)
    vmem = pl.BlockSpec(memory_space=pltpu.VMEM)
    length, owner, slot = (x.reshape(1, opts) for x in (opt_length, opt_owner, opt_slot))
    kept = 2 * width * (2 * rows + n * CAP) + 4 * HD * CAP * (n + 1)
    kept += 2 * rows * kvs * (2 * HD + VR) + 4 * (heads + 1) * (VR + 8) * rows
    state = pl.pallas_call(
        functools.partial(attend, n),
        out_shape=(
            pltpu.VMEM((rows, width), bf16),
            pltpu.VMEM((n, CAP, width), bf16),
            pltpu.VMEM((n, CAP, HD), f32),
            pltpu.VMEM((CAP, HD), f32),
            pltpu.VMEM((rows, width), bf16),
            pltpu.VMEM((rows, 2 * kvs * HD), bf16),
            pltpu.VMEM((kvs, VR, rows), bf16),
            pltpu.VMEM((heads + 1, VR, rows), f32),
            pltpu.VMEM((heads + 1, 8, rows), f32),
        ),
        in_specs=[hbm] * 7,
        out_specs=(vmem,) * 9,
        scratch_shapes=[
            pltpu.VMEM((rows, kvs * HD), bf16),
            pltpu.VMEM((rows, kvs * HD), bf16),
            pltpu.VMEM((kvs, VR, rows), bf16),
            pltpu.VMEM((opts, width), bf16),
            pltpu.VMEM((rows // HALVES, rows), f32),
            pltpu.VMEM((rows // HALVES, rows), f32),
            pltpu.VMEM((rows // HALVES, rows), bf16),
            pltpu.VMEM((rows // HALVES, rows), bf16),
            pltpu.VMEM((16, rows), f32),
            pltpu.VMEM((16, rows), f32),
            pltpu.VMEM((opts, width), bf16),
            pltpu.VMEM((opts, HD), f32),
            pltpu.VMEM((n * CAP, width), bf16),
            pltpu.VMEM((n * CAP, HD), f32),
            pltpu.VMEM((n, CAP, width), bf16),
            pltpu.VMEM((n, CAP, HD), f32),
            pltpu.VMEM((24, opts), jnp.int32),
            dma((3,)), dma((heads // PAIR,)), dma(()), dma(()), dma(()),
            dma((n - 1,)), dma((n - 1,)), dma((n - 1,)), dma((n - 1,)), dma((2,)), dma(()),
            dma((chunks,)), dma((chunks,)), dma((chunks,)),
            dma((n - 1,)), dma((n - 1,)), dma((n - 1,)), dma((n - 1,)),
            dma((n, SPLIT)), dma((n, SPLIT)), dma((n,)), dma((n,)),
            pltpu.SemaphoreType.REGULAR, pltpu.SemaphoreType.REGULAR,
        ],
        compiler_params=pltpu.CompilerParams(
            collective_id=0, has_side_effects=True, vmem_limit_bytes=LIMIT - kept
        ),
        name="star",
    )(ctx_query, ctx_key, ctx_value, opt_query, length, owner, slot)
    return pl.pallas_call(
        functools.partial(merge, n),
        out_shape=(
            jax.ShapeDtypeStruct((rows, width), bf16),
            jax.ShapeDtypeStruct((CAP, width), bf16),
        ),
        in_specs=[vmem] * 9,
        out_specs=(hbm, hbm),
        scratch_shapes=[
            pltpu.VMEM((rows, TAIL * HD), bf16),
            pltpu.VMEM((CAP, width), bf16),
            dma((WRITES,)),
            dma((TAIL // PAIR,)),
            dma(()),
        ],
        compiler_params=pltpu.CompilerParams(vmem_limit_bytes=16 * 1024 * 1024),
        name="merge",
    )(*state)


def solution(mesh):
    return jax.shard_map(
        body,
        mesh=mesh,
        in_specs=(
            P(("groups", "blk"), "head"),
            P(("groups", "blk"), "head"),
            P(("groups", "blk"), "head"),
            P(("groups", "blk"), "head"),
            P("groups"),
            P("groups"),
            P("groups"),
        ),
        out_specs=(P(("groups", "blk"), "head"), P(("groups", "blk"), "head")),
        check_vma=False,
    )
```

```python
import functools
import math

import jax
import jax.numpy as jnp
from jax import lax
from jax.experimental import pallas as pl
from jax.experimental.pallas import tpu as pltpu
from jax.sharding import PartitionSpec as P

HD = 128
HQ = 64
KVH = 8
CAP = 32
GROUP = HQ // KVH
MESH = pl.DeviceIdType.MESH
NEG = -1e30
LN2 = math.log(2.0)
COEF = HD**-0.5 / LN2
PAIR = 2
HALVES = 2
PIECES = 4
VR = HD + 16
PER = GROUP // 2
WRITES = 2
LEAD = 2
SPLIT = 2
TAIL = 6
LIMIT = 65100 * 1024
GREET = 0


def dot_nt(a, b):
    return lax.dot_general(a, b, (((1,), (1,)), ((), ())), preferred_element_type=jnp.float32)


def dot_nn(a, b, precision=None):
    return lax.dot_general(
        a, b, (((1,), (0,)), ((), ())), preferred_element_type=jnp.float32, precision=precision
    )


def staged(count, scores, soften, gather):
    for k in range(count + 2):
        if k < count:
            scores(k)
        if 0 <= k - 1 < count:
            soften(k - 1)
        if 0 <= k - 2 < count:
            gather(k - 2)


def attend(
    n,
    q_hbm, k_hbm, v_hbm, oq_hbm, len_hbm, owner_hbm, slot_hbm,
    ctx_ref, rx_p, rx_s, mine_ref, q_ref, ak_ref, avt_ref, acc_ref, m_ref,
    k_ref, v_ref, vt_ref, oq_ref,
    raw_a, raw_b, prob_a, prob_b, top_a, top_b, part_ref, stat_ref, pbuf, sbuf, up_p, up_s, place_ref,
    place_sem, q_sem, k_sem, v_sem, o_sem,
    oq_send, oq_recv, ou_send, ou_recv, oz_send, oz_recv, ak_send, ak_recv, av_send,
    p_send, p_recv, s_send, s_recv, pu_send, pu_recv, su_send, su_recv, low_sem, near_sem,
):
    me = lax.axis_index("blk")
    rows = q_ref.shape[0]
    heads = q_ref.shape[1] // HD
    kvs = k_ref.shape[1] // HD
    entry = oq_hbm.shape[0]
    opts = oq_ref.shape[0]
    pairs = heads // PAIR
    tile = rows // 2
    span_rows = rows // HALVES
    chunk = span_rows // PIECES
    chunks = kvs * HALVES * PIECES

    def q_copy(i):
        cols = pl.ds(pl.multiple_of(i * PAIR * HD, PAIR * HD), PAIR * HD)
        return pltpu.make_async_copy(q_hbm.at[:, cols], q_ref.at[:, cols], q_sem.at[i])

    k_copy = pltpu.make_async_copy(k_hbm, k_ref, k_sem)
    v_copy = pltpu.make_async_copy(v_hbm, v_ref, v_sem)
    own = pl.ds(pl.multiple_of(me * entry, entry), entry)
    o_copy = pltpu.make_async_copy(oq_hbm, oq_ref.at[own], o_sem)

    place_copies = [
        pltpu.make_async_copy(src, place_ref.at[pl.ds(8 * i, 1)], place_sem.at[i])
        for i, src in enumerate((len_hbm, owner_hbm, slot_hbm))
    ]
    barrier = pltpu.get_barrier_semaphore()
    up = lax.rem(me + 1, n)
    below = lax.rem(me - 1 + n, n)

    @pl.when(me < n - 1)
    def _():
        pl.semaphore_signal(barrier, inc=1, device_id={"blk": up}, device_id_type=MESH)

    @pl.when(me > 0)
    def _():
        pl.semaphore_signal(barrier, inc=1, device_id={"blk": below}, device_id_type=MESH)

    k_copy.start()
    q_copy(0).start()
    v_copy.start()
    for i in range(1, pairs):
        q_copy(i).start()
    o_copy.start()
    for copy in place_copies:
        copy.start()

    def oq_copy(step):
        return pltpu.make_async_remote_copy(
            src_ref=oq_hbm,
            dst_ref=oq_ref.at[own],
            send_sem=oq_send.at[step - 1],
            recv_sem=oq_recv.at[step - 1],
            device_id={"blk": lax.rem(me - step + n, n)},
            device_id_type=MESH,
        )

    def oq_up(step):
        at = lax.rem(me + 1 - step + n, n)
        span = pl.ds(pl.multiple_of(at * entry, entry), entry)
        return pltpu.make_async_remote_copy(
            src_ref=oq_hbm if step == 1 else oq_ref.at[span],
            dst_ref=oq_ref.at[span],
            send_sem=ou_send.at[step - 1],
            recv_sem=ou_recv.at[step - 1],
            device_id={"blk": up},
            device_id_type=MESH,
        )

    def oq_pass(step):
        @pl.when(me > step)
        def _():
            oq_up(step).wait_recv()

        @pl.when((me > step) & (me < n - 1))
        def _():
            oq_up(step + 1).start()

    first_rows = pl.ds(0, entry)

    hub = min(2, n - 1)

    def oq_first(index, to, relay):
        return pltpu.make_async_remote_copy(
            src_ref=oq_ref.at[first_rows] if relay else oq_hbm,
            dst_ref=oq_ref.at[first_rows],
            send_sem=oz_send.at[index],
            recv_sem=oz_recv,
            device_id={"blk": to},
            device_id_type=MESH,
        )

    def head_cols(h):
        return pl.ds(pl.multiple_of(h * HD, HD), HD)

    def anchor_copies(c, first):
        g = c // (HALVES * PIECES)
        r = lax.rem(c, HALVES * PIECES)
        span = pl.ds(pl.multiple_of(r * chunk, chunk), chunk)

        def copy(src, cols, send):
            return pltpu.make_async_remote_copy(
                src_ref=src,
                dst_ref=ak_ref.at[span, cols],
                send_sem=send.at[c],
                recv_sem=ak_recv.at[c],
                device_id={"blk": up},
                device_id_type=MESH,
            )

        if not first:
            both = pl.ds(pl.multiple_of(2 * g * HD, 2 * HD), 2 * HD)
            return (copy(ak_ref.at[span, both], both, ak_send),)
        return (
            copy(k_hbm.at[span, head_cols(g)], head_cols(2 * g), ak_send),
            copy(v_hbm.at[span, head_cols(g)], head_cols(2 * g + 1), av_send),
        )

    def send_anchor(low, high):
        def send(c, carry):
            for copy in anchor_copies(c, True):
                copy.start()
            return carry

        lax.fori_loop(low, high, send, 0)

    def greet():
        @pl.when((me > 0) & (me < n - 1))
        def _():
            pl.semaphore_wait(barrier, 2)

        @pl.when((me == 0) | (me == n - 1))
        def _():
            pl.semaphore_wait(barrier, 1)

        @pl.when(me == 0)
        def _():
            send_anchor(0, LEAD)

        @pl.when(me > 1)
        def _():
            pl.semaphore_wait(low_sem, 1)

        @pl.when((me > 0) & (me < n - 1))
        def _():
            pl.semaphore_signal(low_sem, inc=1, device_id={"blk": up}, device_id_type=MESH)

        @pl.when((me == 1) & (me < n - 1))
        def _():
            pl.semaphore_signal(near_sem, inc=1, device_id={"blk": below}, device_id_type=MESH)

        if n > 2:
            @pl.when(me == 0)
            def _():
                pl.semaphore_wait(near_sem, 1)

        @pl.when(me == 0)
        def _():
            oq_first(0, hub, False).start()
            send_anchor(LEAD, chunks)

        @pl.when((me > 0) & (me < n - 1))
        def _():
            oq_up(1).start()

        for step in range(1, n):
            @pl.when(me >= step)
            def _():
                oq_copy(step).start()

    def forward(c):
        for copy in anchor_copies(c, False):
            copy.wait_recv()

        @pl.when(me < n - 1)
        def _():
            for copy in anchor_copies(c, False):
                copy.start()

    ones = jnp.ones((VR - HD, rows), jnp.bfloat16)
    k_copy.wait()
    v_copy.wait()
    for g in range(kvs):
        vt_ref[g, :HD, :] = v_ref[:, g * HD : (g + 1) * HD].T
        vt_ref[g, HD:, :] = ones
        avt_ref[g, HD:, :] = ones

    causal = lax.broadcasted_iota(jnp.int32, (tile, tile), 0) <= lax.broadcasted_iota(
        jnp.int32, (tile, tile), 1
    )

    def local_heads(hs):
        units = [(h, t) for h in hs for t in range(2)]
        raw, tops, probs = {}, {}, {}

        def scores(u):
            h, t = units[u]
            query = q_ref[pl.ds(t * tile, tile), head_cols(h)]
            score = dot_nt(k_ref[pl.ds(0, (t + 1) * tile), head_cols(h // GROUP)], query)
            parts = [score[j * tile : (j + 1) * tile] for j in range(t + 1)]
            parts[t] = jnp.where(causal, parts[t], NEG)
            top = functools.reduce(jnp.maximum, [jnp.max(x, axis=0, keepdims=True) for x in parts])
            tops[u] = top * COEF
            raw[u] = parts

        def soften(u):
            probs[u] = [jnp.exp2(x * COEF - tops[u]).astype(jnp.bfloat16) for x in raw.pop(u)]

        def gather(u):
            h, t = units[u]
            span = pl.ds(t * tile, tile)
            prob = jnp.concatenate(probs.pop(u), axis=0)
            acc_ref[h, :, span] = dot_nn(vt_ref[h // GROUP, :, pl.ds(0, (t + 1) * tile)], prob)
            m_ref[h, :, span] = jnp.broadcast_to(tops[u], (8, tile))

        staged(len(units), scores, soften, gather)

    def finish(h, span, acc):
        ctx_ref[span, head_cols(h)] = (acc[:HD] * (1.0 / acc[HD : HD + 1])).T.astype(jnp.bfloat16)

    units = heads * HALVES - TAIL
    per = PER

    def unit_place(u):
        block = u // GROUP
        g = block // HALVES
        half = lax.rem(block, HALVES)
        keys = pl.ds(pl.multiple_of(half * span_rows, span_rows), span_rows)
        return g, g * GROUP + lax.rem(u, GROUP), keys

    def unit_scores(u, raw, top):
        g, h, keys = unit_place(jnp.minimum(u, units - 1))
        for t in range(2):
            span = pl.ds(t * tile, tile)
            score = dot_nt(ak_ref[keys, head_cols(2 * g)], q_ref[span, head_cols(h)])
            raw[:, span] = score
            high = jnp.max(score, axis=0, keepdims=True) * COEF
            high = jnp.maximum(high, m_ref[h, pl.ds(0, 1), span])
            top[pl.ds(0, 8), span] = jnp.broadcast_to(high, (8, tile))

    def unit_soften(raw, top, prob):
        for t in range(2):
            span = pl.ds(t * tile, tile)
            high = top[pl.ds(0, 1), span]
            prob[:, span] = jnp.exp2(raw[:, span] * COEF - high).astype(jnp.bfloat16)
        top[pl.ds(8, 8), :] = top[pl.ds(0, 8), :]

    def unit_gather(u, prob, top, last):
        g, h, keys = unit_place(jnp.maximum(u, 0))
        slot = jnp.where(u < 0, heads, h)
        for t in range(2):
            span = pl.ds(t * tile, tile)
            high = top[pl.ds(8, 1), span]
            alpha = jnp.exp2(m_ref[slot, pl.ds(0, 1), span] - high)
            acc = dot_nn(avt_ref[g, :, keys], prob[:, span]) + alpha * acc_ref[slot, :, span]
            if last:
                finish(h, span, acc)
            else:
                acc_ref[slot, :, span] = acc
                m_ref[slot, :, span] = jnp.broadcast_to(high, (8, tile))

    def trip(i, last):
        unit_gather(2 * i - 2, prob_a, top_a, last)
        unit_soften(raw_b, top_b, prob_b)
        unit_scores(2 * i, raw_a, top_a)
        unit_gather(2 * i - 1, prob_b, top_b, last)
        unit_soften(raw_a, top_a, prob_a)
        unit_scores(2 * i + 1, raw_b, top_b)

    for copy in place_copies:
        copy.wait()
    length = place_ref[pl.ds(0, 1), :].astype(jnp.float32)
    dest = place_ref[pl.ds(8, 1), :] * CAP + place_ref[pl.ds(16, 1), :]

    def opt_attend(queries, counts, key, value_t):
        size = queries.shape[0]
        stacked = jnp.concatenate([queries[:, j * HD : (j + 1) * HD] for j in range(GROUP)], axis=0)
        score = dot_nt(key, stacked)
        if counts is not None:
            spot = lax.broadcasted_iota(jnp.int32, score.shape, 0).astype(jnp.float32)
            score = jnp.where(spot < counts, score, NEG)
        top = jnp.max(score, axis=0, keepdims=True) * COEF
        acc = dot_nn(value_t, jnp.exp2(score * COEF - top).astype(jnp.bfloat16))
        total = acc[HD : HD + 1]
        part = acc[:HD] * (1.0 / total)
        stat = top * LN2 + jnp.log(total)
        if counts is not None:
            live = counts > 0.0
            part = jnp.where(live, part, 0.0)
            stat = jnp.where(live, stat, NEG)
        part = part.T.astype(jnp.bfloat16)
        stat = jnp.broadcast_to(stat, (HD, stat.shape[1])).T
        return (
            [part[j * size : (j + 1) * size] for j in range(GROUP)],
            [stat[j * size : (j + 1) * size] for j in range(GROUP)],
        )

    step_rows = min(opts, 64)
    lane_opts = GROUP * step_rows

    def options_group(g):
        lanes = lax.broadcasted_iota(jnp.int32, (step_rows, HD), 1)
        for base in range(0, opts, step_rows):
            span = pl.ds(base, step_rows)
            pick = lax.broadcasted_iota(jnp.int32, (opts, lane_opts), 0) - base
            pick = pick == lax.rem(lax.broadcasted_iota(jnp.int32, (opts, lane_opts), 1), step_rows)
            spread = dot_nn(
                jnp.broadcast_to(length, (8, opts)), pick.astype(jnp.float32), lax.Precision.HIGHEST
            )
            counts = jnp.clip(spread[:1] - (me * rows).astype(jnp.float32), 0.0, float(rows))
            queries = oq_ref[span, pl.ds(g * GROUP * HD, GROUP * HD)]
            parts, tops = opt_attend(queries, counts, k_ref[:, pl.ds(g * HD, HD)], vt_ref[g])
            stats = jnp.zeros((step_rows, HD), jnp.float32) if g == 0 else stat_ref[span, :]
            for j in range(GROUP):
                h = g * GROUP + j
                part_ref[span, pl.ds(h * HD, HD)] = parts[j]
                stats = jnp.where(lanes == h, tops[j], stats)
            stat_ref[span, :] = stats

    slots = lax.broadcasted_iota(jnp.int32, (CAP, opts), 0)
    mine = (slots + me * CAP == dest).astype(jnp.float32)
    mine_ref[...] = jnp.broadcast_to(jnp.sum(mine, axis=1, keepdims=True), (CAP, HD))

    def options_scatter():
        for d in range(n):
            hot = (slots + d * CAP == dest).astype(jnp.float32)
            span = pl.ds(d * CAP, CAP)
            pbuf[span, :] = dot_nn(hot.astype(jnp.bfloat16), part_ref[...]).astype(jnp.bfloat16)
            sbuf[span, :] = dot_nn(hot, stat_ref[...], lax.Precision.HIGHEST)

    def down_copies(step):
        to = lax.rem(me - step + n, n)
        span = pl.ds(pl.multiple_of(to * CAP, CAP), CAP)
        return (
            pltpu.make_async_remote_copy(
                src_ref=pbuf.at[span],
                dst_ref=rx_p.at[me],
                send_sem=p_send.at[step - 1],
                recv_sem=p_recv.at[step - 1],
                device_id={"blk": to},
                device_id_type=MESH,
            ),
            pltpu.make_async_remote_copy(
                src_ref=sbuf.at[span],
                dst_ref=rx_s.at[me],
                send_sem=s_send.at[step - 1],
                recv_sem=s_recv.at[step - 1],
                device_id={"blk": to},
                device_id_type=MESH,
            ),
        )

    share = heads // SPLIT

    def up_copies(d, piece, final):
        span = pl.ds(d * CAP, CAP)
        cols = pl.ds(piece * share * HD, share * HD)
        copies = [
            pltpu.make_async_remote_copy(
                src_ref=pbuf.at[span, cols],
                dst_ref=rx_p.at[me, :, cols] if final else up_p.at[d, :, cols],
                send_sem=pu_send.at[d, piece],
                recv_sem=pu_recv.at[d, piece],
                device_id={"blk": up},
                device_id_type=MESH,
            )
        ]
        if piece == 0:
            copies.append(
                pltpu.make_async_remote_copy(
                    src_ref=sbuf.at[span],
                    dst_ref=rx_s.at[me] if final else up_s.at[d],
                    send_sem=su_send.at[d],
                    recv_sem=su_recv.at[d],
                    device_id={"blk": up},
                    device_id_type=MESH,
                )
            )
        return copies

    def send_down():
        for step in range(n - 1, 0, -1):
            @pl.when(me >= step)
            def _():
                for copy in down_copies(step):
                    copy.start()

    def combine(d):
        span = pl.ds(d * CAP, CAP)
        final = me == d - 1
        for piece in range(SPLIT):
            for copy in up_copies(d, piece, False):
                copy.wait_recv()
            if piece == 0:
                low, own_stat = up_s[d], sbuf[span, :]
                top = jnp.maximum(low, own_stat)
                low, own_stat = jnp.exp(low - top), jnp.exp(own_stat - top)
                total = low + own_stat
                sbuf[span, :] = top + jnp.log(total)
                low, own_stat = low / total, own_stat / total
            for h in range(piece * share, (piece + 1) * share):
                cols = pl.ds(h * HD, HD)
                mixed = low[:, h : h + 1] * up_p[d, :, cols].astype(jnp.float32)
                mixed = mixed + own_stat[:, h : h + 1] * pbuf[span, cols].astype(jnp.float32)
                pbuf[span, cols] = mixed.astype(jnp.bfloat16)

            @pl.when(final)
            def _():
                for copy in up_copies(d, piece, True):
                    copy.start()

            @pl.when(jnp.logical_not(final))
            def _():
                for copy in up_copies(d, piece, False):
                    copy.start()

    def send_up_first():
        for d in range(n - 1, 2, -1):
            for piece in range(SPLIT):
                for copy in up_copies(d, piece, False):
                    copy.start()

    def send_up_rest():
        for d in range(n - 1, 2, -1):
            @pl.when(me < d)
            def _():
                combine(d)

    def send_up_last():
        for piece in range(SPLIT):
            for copy in up_copies(hub, piece, True):
                copy.start()

    def options_anchor(g, key_of, value_of, stride):
        hot = mine.astype(jnp.bfloat16)
        lanes = lax.broadcasted_iota(jnp.int32, (CAP, HD), 1)
        queries = dot_nn(hot, oq_ref[:, pl.ds(pl.multiple_of(g * GROUP * HD, GROUP * HD), GROUP * HD)]).astype(jnp.bfloat16)
        parts, tops = opt_attend(queries, None, key_of[:, head_cols(stride * g)], value_of[g])
        stats = rx_s[0]
        for j in range(GROUP):
            h = g * GROUP + j
            rx_p[0, :, head_cols(h)] = parts[j]
            stats = jnp.where(lanes == h, tops[j], stats)
        rx_s[0] = stats

    @pl.when(me == 0)
    def _():
        greet()

    def local_pair(i, carry):
        q_copy(i).wait()
        local_heads([i * PAIR + j for j in range(PAIR)])

        @pl.when((i == GREET) & (me > 0))
        def _():
            greet()

        @pl.when(i == max(pairs - 3, 0))
        def _():
            oq_pass(1)

        @pl.when((i >= pairs - 2) & (me == 1) & (me < n - 1))
        def _():
            forward(i - (pairs - 2))

        return carry

    lax.fori_loop(0, pairs, local_pair, 0)

    relay_down = (me == hub) & (me > 1)
    relay_up = (me >= hub) & (me < n - 1)

    def oq_wait():
        o_copy.wait()

        @pl.when(me > 0)
        def _():
            oq_first(0, up, True).wait_recv()

        @pl.when(relay_up)
        def _():
            oq_first(0, up, True).start()

        @pl.when(relay_down)
        def _():
            oq_first(1, below, True).start()

        for step in range(2, n - 1):
            oq_pass(step)
        for step in range(1, n):
            @pl.when(me + step < n)
            def _():
                oq_copy(step).wait_recv()

    @pl.when(me == 0)
    def _():
        oq_wait()

        def whole(h, carry):
            for t in range(2):
                span = pl.ds(t * tile, tile)
                finish(h, span, acc_ref[h, :, span])
            return carry

        lax.fori_loop(0, heads, whole, 0)
        rx_s[0] = jnp.zeros_like(rx_s[0])
        for g in range(kvs):
            options_anchor(g, k_ref, vt_ref, 1)

    @pl.when(me > 0)
    def _():

        def forward_range(low, high):
            def one(c, carry):
                forward(c)
                return carry

            lax.fori_loop(low, high, one, 0)

        @pl.when(me == 1)
        def _():
            forward_range(jnp.where(me < n - 1, 2, 0), PIECES)

        steps = units // 2 + 1
        early = min(PER + 1, steps - 1)
        sent = min(early + PIECES, steps - 1)
        closing = min(chunks - PIECES, steps - 1)

        def forward_early(c):
            @pl.when((me == 1) & (c < chunks))
            def _():
                forward(c)

        def options_all():
            oq_wait()
            for g in range(kvs):
                options_group(g)
                forward_early(PIECES + early + g)
            options_scatter()
            forward_early(PIECES + early + kvs)
            send_down()
            own_slots = pl.ds(pl.multiple_of(me * CAP, CAP), CAP)
            rx_p[me] = pbuf[own_slots, :]
            rx_s[me] = sbuf[own_slots, :]
            for b in range(1, n - 2):
                @pl.when(b < me - 1)
                def _():
                    rx_p[b] = jnp.zeros_like(rx_p[b])
                    rx_s[b] = jnp.full_like(rx_s[b], NEG)


            @pl.when(me > 1)
            def _():
                forward_range(0, PIECES)

        turn = jnp.where(me == 1, early, 0)
        rx_s[0] = jnp.zeros_like(rx_s[0])

        def turn_values(u):
            g, _, keys = unit_place(u)
            avt_ref[g, :HD, keys] = ak_ref[keys, head_cols(2 * g + 1)].T

        def anchor_step(i, carry):
            @pl.when(i == turn)
            def _():
                options_all()

            @pl.when((lax.rem(i, per) == 0) & (2 * i < units))
            def _():
                turn_values(2 * i)

            last = lax.rem((jnp.maximum(i, 1) - 1) // per, HALVES) == HALVES - 1

            @pl.when(last)
            def _():
                trip(i, True)

            @pl.when(jnp.logical_not(last))
            def _():
                trip(i, False)

            following = PIECES + i + jnp.where((me == 1) & (i >= early), kvs + 1, 0)

            @pl.when(following < chunks)
            def _():
                forward(following)

            @pl.when((me == 1) & (i == sent))
            def _():
                send_up_first()

            @pl.when((me == 1) & (me < n - 1) & (i == max(closing, sent)))
            def _():
                send_up_last()

            @pl.when((me > 1) & (me < n - 1) & (i == closing))
            def _():
                send_up_rest()

            @pl.when((lax.rem(i, per * HALVES) == per + 1) & (me == n - 1))
            def _():
                options_anchor(i // (per * HALVES), ak_ref, avt_ref, 2)

            return carry

        lax.fori_loop(0, steps, anchor_step, 0)

        def options_rest(g, carry):
            options_anchor(g, ak_ref, avt_ref, 2)
            return carry

        @pl.when(me < n - 1)
        def _():
            lax.fori_loop(0, kvs, options_rest, 0)

    for step in range(1, n):
        @pl.when(me + step < n)
        def _():
            for copy in down_copies(step):
                copy.wait_recv()

    for d in range(2, n):
        @pl.when(me == d)
        def _():
            for piece in range(SPLIT):
                for copy in up_copies(d, piece, True):
                    copy.wait_recv()

    for step in range(1, n):
        @pl.when(me >= step)
        def _():
            oq_copy(step).wait_send()

        @pl.when((me >= step) & (me < n - 1))
        def _():
            oq_up(step).wait_send()

    @pl.when((me == 0) | relay_up)
    def _():
        oq_first(0, up, True).wait_send()

    @pl.when(relay_down)
    def _():
        oq_first(1, below, True).wait_send()

    @pl.when(me == 0)
    def _():
        def drain(c, carry):
            for copy in anchor_copies(c, True):
                copy.wait_send()
            return carry

        lax.fori_loop(0, chunks, drain, 0)

    @pl.when((me > 0) & (me < n - 1))
    def _():
        def drain(c, carry):
            for copy in anchor_copies(c, False):
                copy.wait_send()
            return carry

        lax.fori_loop(0, chunks, drain, 0)

    for step in range(1, n):
        @pl.when(me >= step)
        def _():
            for copy in down_copies(step):
                copy.wait_send()

    for d in range(2, n):
        @pl.when((me > 0) & (me < d))
        def _():
            for piece in range(SPLIT):
                for copy in up_copies(d, piece, False):
                    copy.wait_send()


def merge(
    n,
    ctx_ref, rx_p, rx_s, mine_ref, q_ref, ak_ref, avt_ref, acc_ref, m_ref,
    ctx_hbm, opt_hbm,
    tail_ref, opt_ref, sem, tail_sem, opt_sem,
):
    me = lax.axis_index("blk")
    rows, width = ctx_ref.shape
    heads = width // HD
    tile = rows // 2
    base = heads - TAIL
    g = heads // GROUP - 1
    span_rows = rows // HALVES
    keys = pl.ds((HALVES - 1) * span_rows, span_rows)
    part = rows // WRITES

    def early_copies():
        return [
            pltpu.make_async_copy(
                ctx_ref.at[pl.ds(i * part, part), pl.ds(0, base * HD)],
                ctx_hbm.at[pl.ds(i * part, part), pl.ds(0, base * HD)],
                sem.at[i],
            )
            for i in range(WRITES)
        ]

    def tail_copy(i, src):
        cols = pl.ds(i * PAIR * HD, PAIR * HD)
        return pltpu.make_async_copy(
            src.at[:, cols if src is tail_ref else pl.ds((base + i * PAIR) * HD, PAIR * HD)],
            ctx_hbm.at[:, pl.ds((base + i * PAIR) * HD, PAIR * HD)],
            tail_sem.at[i],
        )

    if base:
        for copy in early_copies():
            copy.start()

    top = rx_s[0]
    for b in range(1, n):
        top = jnp.maximum(top, rx_s[b])
    weights = [jnp.exp(rx_s[b] - top) for b in range(n)]
    scale = 1.0 / functools.reduce(jnp.add, weights)
    weights = [x * scale for x in weights]
    occupied = mine_ref[...] > 0.0

    opt_copy = pltpu.make_async_copy(opt_ref, opt_hbm, opt_sem)

    def merge_head(h):
        cols = pl.ds(h * HD, HD)
        merged = jnp.zeros((CAP, HD), jnp.float32)
        for b in range(n):
            merged = merged + weights[b][:, h : h + 1] * rx_p[b, :, cols].astype(jnp.float32)
        opt_ref[:, cols] = jnp.where(occupied, merged, 0.0).astype(jnp.bfloat16)

    @pl.when(me == 0)
    def _():
        for i in range(TAIL // PAIR):
            tail_copy(i, ctx_ref).start()
        for h in range(heads):
            merge_head(h)
        opt_copy.start()

    @pl.when(me > 0)
    def _():
        units = [(j, t) for j in range(TAIL) for t in range(2)]
        raw, tops, probs = {}, {}, {}

        def scores(u):
            j, t = units[u]
            span = pl.ds(t * tile, tile)
            query = q_ref[span, pl.ds((base + j) * HD, HD)]
            raw[u] = dot_nt(ak_ref[keys, pl.ds(2 * g * HD, HD)], query)
            high = jnp.max(raw[u], axis=0, keepdims=True) * COEF
            tops[u] = jnp.maximum(high, m_ref[base + j, pl.ds(0, 1), span])

        def soften(u):
            probs[u] = jnp.exp2(raw.pop(u) * COEF - tops[u]).astype(jnp.bfloat16)

        def gather(u):
            j, t = units[u]
            span = pl.ds(t * tile, tile)
            alpha = jnp.exp2(m_ref[base + j, pl.ds(0, 1), span] - tops[u])
            acc = dot_nn(avt_ref[g, :, keys], probs.pop(u)) + alpha * acc_ref[base + j, :, span]
            out = (acc[:HD] * (1.0 / acc[HD : HD + 1])).T.astype(jnp.bfloat16)
            tail_ref[span, pl.ds(j * HD, HD)] = out
            half = len(units) // 2
            for h in range(min(u, half) * heads // half, min(u + 1, half) * heads // half):
                merge_head(h)
            if u == half - 1:
                opt_copy.start()
            if t == 1 and j % PAIR == PAIR - 1:
                tail_copy(j // PAIR, tail_ref).start()

        staged(len(units), scores, soften, gather)

    if base:
        for copy in early_copies():
            copy.wait()
    for i in range(TAIL // PAIR):
        tail_copy(i, ctx_ref).wait()
    opt_copy.wait()


def body(ctx_query, ctx_key, ctx_value, opt_query, opt_owner, opt_slot, opt_length):
    n = lax.axis_size("blk")
    rows, width = ctx_query.shape
    heads = width // HD
    kvs = ctx_key.shape[1] // HD
    opts = opt_length.shape[0]
    chunks = HALVES * PIECES * kvs
    bf16, f32 = jnp.bfloat16, jnp.float32
    dma = pltpu.SemaphoreType.DMA
    hbm = pl.BlockSpec(memory_space=pltpu.HBM)
    vmem = pl.BlockSpec(memory_space=pltpu.VMEM)
    length, owner, slot = (x.reshape(1, opts) for x in (opt_length, opt_owner, opt_slot))
    kept = 2 * width * (2 * rows + n * CAP) + 4 * HD * CAP * (n + 1)
    kept += 2 * rows * kvs * (2 * HD + VR) + 4 * (heads + 1) * (VR + 8) * rows
    state = pl.pallas_call(
        functools.partial(attend, n),
        out_shape=(
            pltpu.VMEM((rows, width), bf16),
            pltpu.VMEM((n, CAP, width), bf16),
            pltpu.VMEM((n, CAP, HD), f32),
            pltpu.VMEM((CAP, HD), f32),
            pltpu.VMEM((rows, width), bf16),
            pltpu.VMEM((rows, 2 * kvs * HD), bf16),
            pltpu.VMEM((kvs, VR, rows), bf16),
            pltpu.VMEM((heads + 1, VR, rows), f32),
            pltpu.VMEM((heads + 1, 8, rows), f32),
        ),
        in_specs=[hbm] * 7,
        out_specs=(vmem,) * 9,
        scratch_shapes=[
            pltpu.VMEM((rows, kvs * HD), bf16),
            pltpu.VMEM((rows, kvs * HD), bf16),
            pltpu.VMEM((kvs, VR, rows), bf16),
            pltpu.VMEM((opts, width), bf16),
            pltpu.VMEM((rows // HALVES, rows), f32),
            pltpu.VMEM((rows // HALVES, rows), f32),
            pltpu.VMEM((rows // HALVES, rows), bf16),
            pltpu.VMEM((rows // HALVES, rows), bf16),
            pltpu.VMEM((16, rows), f32),
            pltpu.VMEM((16, rows), f32),
            pltpu.VMEM((opts, width), bf16),
            pltpu.VMEM((opts, HD), f32),
            pltpu.VMEM((n * CAP, width), bf16),
            pltpu.VMEM((n * CAP, HD), f32),
            pltpu.VMEM((n, CAP, width), bf16),
            pltpu.VMEM((n, CAP, HD), f32),
            pltpu.VMEM((24, opts), jnp.int32),
            dma((3,)), dma((heads // PAIR,)), dma(()), dma(()), dma(()),
            dma((n - 1,)), dma((n - 1,)), dma((n - 1,)), dma((n - 1,)), dma((2,)), dma(()),
            dma((chunks,)), dma((chunks,)), dma((chunks,)),
            dma((n - 1,)), dma((n - 1,)), dma((n - 1,)), dma((n - 1,)),
            dma((n, SPLIT)), dma((n, SPLIT)), dma((n,)), dma((n,)),
            pltpu.SemaphoreType.REGULAR, pltpu.SemaphoreType.REGULAR,
        ],
        compiler_params=pltpu.CompilerParams(
            collective_id=0, has_side_effects=True, vmem_limit_bytes=LIMIT - kept
        ),
        name="star",
    )(ctx_query, ctx_key, ctx_value, opt_query, length, owner, slot)
    return pl.pallas_call(
        functools.partial(merge, n),
        out_shape=(
            jax.ShapeDtypeStruct((rows, width), bf16),
            jax.ShapeDtypeStruct((CAP, width), bf16),
        ),
        in_specs=[vmem] * 9,
        out_specs=(hbm, hbm),
        scratch_shapes=[
            pltpu.VMEM((rows, TAIL * HD), bf16),
            pltpu.VMEM((CAP, width), bf16),
            dma((WRITES,)),
            dma((TAIL // PAIR,)),
            dma(()),
        ],
        compiler_params=pltpu.CompilerParams(vmem_limit_bytes=16 * 1024 * 1024),
        name="merge",
    )(*state)


def solution(mesh):
    return jax.shard_map(
        body,
        mesh=mesh,
        in_specs=(
            P(("groups", "blk"), "head"),
            P(("groups", "blk"), "head"),
            P(("groups", "blk"), "head"),
            P(("groups", "blk"), "head"),
            P("groups"),
            P("groups"),
            P("groups"),
        ),
        out_specs=(P(("groups", "blk"), "head"), P(("groups", "blk"), "head")),
        check_vma=False,
    )
```
